256 devices in a mesh: gx: 32 (over y_lo, z, core), gy: 8 (over y_hi, x).
Axes of the slice: x: 4, y: 4 (y_hi: 2, y_lo: 2; y = y_hi * 2 + y_lo), z: 8, core: 2. Of those that a mesh axis runs over, the one named last changes fastest.
Arguments:
- fields: float32 [5, 1, 4096, 4096], P(None, None, 'gx', 'gy'), may hold values from -5 to 5
- metric_x: float32 [4096], P('gx'), may hold values from 0.5 to 2
- metric_y: float32 [4096], P('gy'), may hold values from 0.5 to 2
Outputs:
- first_x: float32 [5, 1, 4096, 4096], P(None, None, 'gx', 'gy')
- second_x: float32 [5, 1, 4096, 4096], P(None, None, 'gx', 'gy')
- first_y: float32 [5, 1, 4096, 4096], P(None, None, 'gx', 'gy')
- second_y: float32 [5, 1, 4096, 4096], P(None, None, 'gx', 'gy')
The draws below stay inside these ranges and needn't reach their ends.
All inputs are finite; a program needn't handle non-finite values.
Results may differ from the reference program's by a relative error of at most 0.0001.
Values sent between devices are 32-bit elements; how exact they have to be, the bound alone decides.
A program may use at most 128 MiB of HBM per device.

```python
import math
import jax
import jax.numpy as jnp
from jax import lax

FIELDS = 5
NZ = 1
NX = 4096
NY = 4096


def draw_fields(key, part):
    shape = (FIELDS, NZ, NX, NY)
    return jnp.clip(jax.random.normal(key, shape, jnp.float32), -5.0, 5.0)


def steps_of(key, extent, pieces, least, high):
    def one(position, blocks):
        heights = jax.random.uniform(jax.random.fold_in(jax.random.fold_in(key, 6), position), (blocks,), jnp.float32, least / len(pieces), high / len(pieces))
        return jnp.repeat(jnp.exp(heights), extent[position] // blocks).reshape((-1,) + (1,) * (len(extent) - position - 1))

    loudness = one(*pieces[0])
    for cut in pieces[1:]:
        loudness = loudness * one(*cut)
    return loudness


def setup_inputs(seed: int = 0) -> dict:
    keys = jax.random.split(jax.random.key(seed), 4)
    fields = draw_fields(jax.random.fold_in(keys[3], 71), 0)
    metric_x = jnp.clip(jnp.exp(math.log(2.0) - 1.3862944 * jax.random.uniform(keys[1], (NX,), jnp.float32) ** steps_of(keys[1], (NX,), ((0, 32),), -0.2, 0.2)), 0.5, 2.0)
    metric_y = jnp.clip(jnp.exp(math.log(2.0) - 1.3862944 * jax.random.uniform(keys[2], (NY,), jnp.float32) ** steps_of(keys[2], (NY,), ((0, 8),), -0.2, 0.2)), 0.5, 2.0)
    return {"fields": fields, "metric_x": metric_x, "metric_y": metric_y}


def shifted(values, offset, along):
    return jnp.roll(values, -offset, axis=along)


def first_side(values, metric, along):
    core = (7.0 / 9.0) * (shifted(values, 1, along) - shifted(values, -1, along)) + (1.0 / 36.0) * (shifted(values, 2, along) - shifted(values, -2, along))
    return metric * core


def second_side(values, metric, along):
    twice = 2.0 * values
    core = (12.0 / 11.0) * (shifted(values, 1, along) - twice + shifted(values, -1, along)) + (3.0 / 44.0) * (shifted(values, 2, along) - twice + shifted(values, -2, along))
    return metric * metric * core


def cyclic_solve(right, alpha, along):
    count = right.shape[along]
    waves = jnp.arange(count).astype(right.dtype)
    divisor = 1.0 + 2.0 * alpha * jnp.cos(2.0 * jnp.pi * waves / count)
    dims = [1, 1]
    dims[along] = count
    spectrum = jnp.fft.fft(right, axis=along) / divisor.reshape(dims)
    return jnp.real(jnp.fft.ifft(spectrum, axis=along)).astype(right.dtype)


def plane_outputs(plane, scale_x, scale_y):
    first_x = cyclic_solve(first_side(plane, scale_x, 0), 1.0 / 3.0, 0)
    second_x = cyclic_solve(second_side(plane, scale_x, 0), 2.0 / 11.0, 0)
    first_y = cyclic_solve(first_side(plane, scale_y, 1), 1.0 / 3.0, 1)
    second_y = cyclic_solve(second_side(plane, scale_y, 1), 2.0 / 11.0, 1)
    return first_x, second_x, first_y, second_y


def reference(fields, metric_x, metric_y):
    scale_x = metric_x[:, None]
    scale_y = metric_y[None, :]
    planes = fields.reshape(FIELDS * NZ, NX, NY)
    results = lax.map(lambda plane: plane_outputs(plane, scale_x, scale_y), planes)
    first_x = results[0].reshape(FIELDS, NZ, NX, NY)
    second_x = results[1].reshape(FIELDS, NZ, NX, NY)
    first_y = results[2].reshape(FIELDS, NZ, NX, NY)
    second_y = results[3].reshape(FIELDS, NZ, NX, NY)
    return first_x, second_x, first_y, second_y
```

```python
import functools

import jax
import jax.numpy as jnp
import numpy as np
from jax import lax
from jax.experimental import pallas as pl
from jax.experimental.pallas import tpu as pltpu
from jax.sharding import PartitionSpec as P

MESH = pl.DeviceIdType.MESH
F32 = jnp.float32
BF16 = jnp.bfloat16

ALPHA = (1.0 / 3.0, 2.0 / 11.0)
NEAR = (7.0 / 9.0, 12.0 / 11.0 + 6.0 / 44.0)
FAR = (1.0 / 36.0, 3.0 / 44.0)
RHO = tuple(-(1.0 - np.sqrt(1.0 - 4.0 * a * a)) / (2.0 * a) for a in ALPHA)
GAIN = tuple(1.0 / np.sqrt(1.0 - 4.0 * a * a) for a in ALPHA)


def flushed(table):
    table = np.asarray(table, np.float64)
    return np.where(np.abs(table) < np.finfo(np.float32).tiny, 0.0, table)


def halves(table):
    table = flushed(table).astype(np.float32)
    high = table.astype(jnp.bfloat16)
    low = (table - high.astype(np.float32)).astype(jnp.bfloat16)
    return high, low


def green(distance, which):
    return GAIN[which] * np.power(RHO[which], np.abs(distance))


def line_tables(count):
    cells = np.arange(count)
    out = [halves(green(cells[:, None] - cells[None, :], w)) for w in range(2)]
    return np.stack([np.stack(pair) for pair in out])


def window_tables():
    rows = np.arange(512)[:, None]
    cols = np.arange(256)[None, :]
    out = [halves(green(rows - 128 - cols, w)) for w in range(2)]
    return np.stack([np.stack(pair) for pair in out])


def edge_rows(count):
    cells = np.arange(count)
    out = np.zeros((24, count))
    for w in range(2):
        out[2 * w] = green(count - 1 - cells, w)
        out[2 * w + 1] = green(cells, w)
        out[8 + 2 * w : 10 + 2 * w] = NEAR[w]
        out[16 + 2 * w : 18 + 2 * w] = FAR[w]
    return flushed(out).astype(np.float32)


def face_columns(count, which):
    cells = np.arange(count)
    out = np.zeros((count, 4))
    rho, fix = RHO[which], GAIN[which] * (RHO[which] - 1.0 / RHO[which])
    out[:, 0] = np.power(rho, cells)
    out[0, 1] = fix
    out[:, 2] = np.power(rho, count - 1 - cells)
    out[count - 1, 3] = fix
    return out


def face_tables_x(fields, count):
    tables = np.zeros((2, fields * count, 128), jnp.bfloat16)
    for w in range(2):
        high, low = halves(face_columns(count, w))
        for k in range(fields):
            for v in range(4):
                rows = slice(k * count, (k + 1) * count)
                tables[w, rows, 8 * v + k] = high[:, v]
                tables[w, rows, 32 + 8 * v + k] = low[:, v]
                tables[w, rows, 64 + 8 * v + k] = high[:, v]
    return tables


def face_tables_y(count):
    tables = np.zeros((256, 4 * count), jnp.bfloat16)
    for w in range(2):
        high, low = halves(face_columns(count, w))
        for v in range(4):
            cols = slice((2 * w + v // 2) * count, (2 * w + v // 2 + 1) * count)
            row = 32 * w + 8 * v
            tables[row, cols] = high[:, v]
            tables[64 + row, cols] = high[:, v]
            tables[128 + row, cols] = low[:, v]
    return tables


def split(value):
    high = value.astype(BF16)
    return high, (value - high.astype(F32)).astype(BF16)


def dot(a, b):
    return jnp.dot(a, b, preferred_element_type=F32)


def right_sides(f, scale, along):
    count = f.shape[along]
    place = lax.broadcasted_iota(jnp.int32, f.shape, along)
    inside = (place > 0) & (place < count - 1)
    after = pltpu.roll(f, count - 1, along)
    before = pltpu.roll(f, 1, along)
    d = jnp.where(inside, after - before, 0.0)
    e = jnp.where(inside, (after - (f + f)) + before, 0.0)
    out = []
    for which, value in ((0, d), (1, e)):
        weight = scale if which == 0 else scale * scale
        sides = pltpu.roll(value, count - 1, along) + pltpu.roll(value, 1, along)
        out.append(weight * (NEAR[which] * value + FAR[which] * sides))
    return out


def edge_weights(table, metric):
    count = metric.shape[1]
    row = lax.broadcasted_iota(jnp.int32, (8, count), 0)
    lane = lax.broadcasted_iota(jnp.int32, (8, count), 1)
    m = jnp.broadcast_to(metric, (8, count))
    base = table[0:8] * jnp.where(row < 2, m, m * m)
    out = table[8:16] * base + table[16:24] * (pltpu.roll(base, 1, 1) + pltpu.roll(base, count - 1, 1))
    return jnp.where((lane > 0) & (lane < count - 1), out, 0.0)


def exchange(
    nx, ny, f_hbm, mx_hbm, my_hbm, edge_hbm, tx_hbm, ty_hbm,
    ux1, ux2, uy1, uy2, sx, sy, hx, hy,
    f, mx, my, edge, tx, ty, pack, column, load, send, recv,
):
    fields, rows, cols = f.shape
    ix, iy = lax.axis_index("gx"), lax.axis_index("gy")
    peers = (
        {"gx": lax.rem(ix + 1, nx)},
        {"gx": lax.rem(ix + nx - 1, nx)},
        {"gy": lax.rem(iy + 1, ny)},
        {"gy": lax.rem(iy + ny - 1, ny)},
    )
    barrier = pltpu.get_barrier_semaphore()
    for peer in peers:
        pl.semaphore_signal(barrier, inc=1, device_id=peer, device_id_type=MESH)
    loads = [
        pltpu.make_async_copy(mx_hbm, mx, load.at[0]),
        pltpu.make_async_copy(my_hbm, my, load.at[1]),
        pltpu.make_async_copy(edge_hbm, edge, load.at[2]),
    ]
    loads += [pltpu.make_async_copy(f_hbm.at[k, 0], f.at[k], load.at[5 + k]) for k in range(fields)]
    loads += [pltpu.make_async_copy(tx_hbm, tx, load.at[3]), pltpu.make_async_copy(ty_hbm, ty, load.at[4])]
    for copy in loads:
        copy.start()

    lane = lax.broadcasted_iota(jnp.int32, (rows, 128), 1)
    for copy in loads[:3]:
        copy.wait()
    table = edge[...]
    scale_x = mx[...]
    along_x = jnp.broadcast_to(scale_x, (rows, rows)).T
    weights_x = edge_weights(table, scale_x)
    weights_x = jnp.concatenate([weights_x, jnp.zeros((rows - 8, rows), F32)], axis=0).T
    last1, first1, last2, first2 = (
        jnp.broadcast_to(weights_x[:, n : n + 1], (rows, 128)) for n in range(4)
    )
    for n, value in enumerate((last1, first1, last2, first2)):
        column[n] = value
    column[4] = along_x
    right_block, left_block = my[:, cols - 128 : cols], my[:, 0:128]
    weights_r = edge_weights(table, right_block)
    weights_l = edge_weights(table, left_block)

    for side in range(2):
        sx[side] = jnp.zeros((32, cols), F32)
    metric_row = jnp.broadcast_to(
        jnp.concatenate([along_x[0:2], along_x[rows - 2 : rows]], axis=0)[:, 0:1], (4, cols)
    )
    sx[0, 5:6, :] = metric_row[2:3]
    sx[0, 13:14, :] = metric_row[3:4]
    sx[1, 5:6, :] = metric_row[0:1]
    sx[1, 13:14, :] = metric_row[1:2]

    def place(tile, spot, value):
        return jnp.where(lane == spot, jnp.broadcast_to(value, tile.shape), tile)

    tile = jnp.zeros((rows, 128), F32)
    tile = place(tile, 5, right_block[:, 126:127])
    tile = place(tile, 13, right_block[:, 127:128])
    tile = place(tile, 37, left_block[:, 0:1])
    tile = place(tile, 45, left_block[:, 1:2])
    pack[...] = tile

    wide = [jnp.concatenate([column[n]] * (cols // 128), axis=1) for n in range(4)]
    for k in range(fields):
        loads[3 + k].wait()
        value = f[k]
        after, before = pltpu.roll(value, rows - 1, 0), pltpu.roll(value, 1, 0)
        d = after - before
        e = (after - (value + value)) + before
        sx[0, k : k + 1, :] = value[rows - 2 : rows - 1]
        sx[0, 8 + k : 9 + k, :] = value[rows - 1 : rows]
        sx[1, k : k + 1, :] = value[0:1]
        sx[1, 8 + k : 9 + k, :] = value[1:2]
        sx[0, 16 + k : 17 + k, :] = jnp.sum(d * wide[0], axis=0, keepdims=True)
        sx[1, 16 + k : 17 + k, :] = jnp.sum(d * wide[1], axis=0, keepdims=True)
        sx[0, 24 + k : 25 + k, :] = jnp.sum(e * wide[2], axis=0, keepdims=True)
        sx[1, 24 + k : 25 + k, :] = jnp.sum(e * wide[3], axis=0, keepdims=True)

        tile = pack[...]
        for side in range(2):
            block = value[:, cols - 128 : cols] if side == 0 else value[:, 0:128]
            weights = weights_r if side == 0 else weights_l
            after, before = pltpu.roll(block, 127, 1), pltpu.roll(block, 1, 1)
            d = after - before
            e = (after - (block + block)) + before
            near = 126 if side == 0 else 0
            tile = place(tile, 32 * side + k, block[:, near : near + 1])
            tile = place(tile, 32 * side + 8 + k, block[:, near + 1 : near + 2])
            one = jnp.sum(d * weights[side : side + 1], axis=1, keepdims=True)
            two = jnp.sum(e * weights[2 + side : 3 + side], axis=1, keepdims=True)
            tile = place(tile, 32 * side + 16 + k, one)
            tile = place(tile, 32 * side + 24 + k, two)
        pack[...] = tile

    turned = pack[...].T
    sy[0] = turned[0:32]
    sy[1] = turned[32:64]
    pl.semaphore_wait(barrier, 4)
    copies = []
    for n, peer in enumerate(peers):
        source, target = (sx, hx) if n < 2 else (sy, hy)
        copy = pltpu.make_async_remote_copy(
            src_ref=source.at[n % 2],
            dst_ref=target.at[n % 2],
            send_sem=send.at[n],
            recv_sem=recv.at[n],
            device_id=peer,
            device_id_type=MESH,
        )
        copy.start()
        copies.append(copy)

    loads[3 + fields].wait()
    loads[4 + fields].wait()
    scale_x = jnp.concatenate([column[4]] * (cols // 128), axis=1)
    scale_y = jnp.broadcast_to(my[...], (rows, cols))

    def solve(k, carry):
        value = f[k]
        for which, (right, out) in enumerate(zip(right_sides(value, scale_x, 0), (ux1, ux2))):
            high, low = split(right)
            out[k] = dot(tx[which, 0], high) + dot(tx[which, 0], low) + dot(tx[which, 1], high)
        for which, (right, out) in enumerate(zip(right_sides(value, scale_y, 1), (uy1, uy2))):
            high, low = split(right)
            for half in range(2):
                window = slice(128 * half, 128 * half + 384)
                part = slice(128 - 128 * half, 512 - 128 * half)
                out[k, :, 256 * half : 256 * half + 256] = (
                    dot(high[:, window], ty[which, 0, part])
                    + dot(low[:, window], ty[which, 0, part])
                    + dot(high[:, window], ty[which, 1, part])
                )
        return carry

    lax.fori_loop(0, fields, solve, 0)
    for copy in copies:
        copy.wait()


def face_values(own, far, side):
    near = own[1 - side]
    a, b = near[0:8], near[8:16]
    inner0, inner1 = (a, b) if side == 0 else (b, a)
    metric0, metric1 = (near[5:6], near[13:14]) if side == 0 else (near[13:14], near[5:6])
    there = far[side]
    a, b = there[0:8], there[8:16]
    outer1, outer2 = (b, a) if side == 0 else (a, b)
    beyond1, beyond2 = (there[13:14], there[5:6]) if side == 0 else (there[5:6], there[13:14])
    sign = 1.0 if side == 0 else -1.0
    differences = (
        (sign * (inner0 - outer2), sign * (inner1 - outer1)),
        ((inner0 - (outer1 + outer1)) + outer2, (inner1 - (inner0 + inner0)) + outer1),
    )
    out = []
    for which, (over, here) in enumerate(differences):
        near_by, far_by, rho, gain = NEAR[which], FAR[which], RHO[which], GAIN[which]
        m0, m1, b1, b2 = (
            (metric0, metric1, beyond1, beyond2)
            if which == 0
            else (metric0 * metric0, metric1 * metric1, beyond1 * beyond1, beyond2 * beyond2)
        )
        carry = there[16 + 8 * which : 24 + 8 * which]
        carry = carry + gain * (rho * far_by * (b2 * over) + b1 * (near_by * over + far_by * here))
        zero = m0 * (near_by * here + far_by * over)
        one = (far_by * m1) * here
        out.append((rho * carry + gain * zero + (gain / rho) * one, one))
    return out


def join(
    ux1, ux2, uy1, uy2, sx, sy, hx, hy, cx, cy,
    ox1, ox2, oy1, oy2, stage_x, stage_y, done,
):
    fields, rows, cols = ux1.shape
    middle = slice(128, cols - 128)
    copies = []

    def put(source, target):
        copy = pltpu.make_async_copy(source, target, done.at[len(copies)])
        copy.start()
        copies.append(copy)

    for part, out in ((uy1, oy1), (uy2, oy2)):
        for k in range(fields):
            put(part.at[k, :, middle], out.at[k, 0, :, middle])

    own, far = (sx[0], sx[1]), (hx[0], hx[1])
    left, right = face_values(own, far, 0), face_values(own, far, 1)
    for which, (part, out) in enumerate(((ux1, ox1), (ux2, ox2))):
        high, low = split(jnp.concatenate([*left[which], *right[which]], axis=0))
        stack = jnp.concatenate([high, high, low], axis=0)
        for k in range(fields):
            lhs = cx[which, rows * k : rows * (k + 1), 0:96]
            stage_x[which, k] = part[k] + dot(lhs, stack)
            put(stage_x.at[which, k], out.at[k, 0])

    own, far = (sy[0], sy[1]), (hy[0], hy[1])
    left, right = face_values(own, far, 0), face_values(own, far, 1)
    values = jnp.concatenate([*left[0], *right[0], *left[1], *right[1]], axis=0)
    high = values.astype(BF16).astype(F32)
    turned = jnp.concatenate([high, values - high], axis=0).T
    for k in range(fields):
        lhs = (turned if k == 0 else pltpu.roll(turned, 128 - k, 1)).astype(BF16)
        both = dot(jnp.concatenate([lhs, lhs], axis=1), cy[...])
        for which, (part, out) in enumerate(((uy1, oy1), (uy2, oy2))):
            for side in range(2):
                place = slice(0, 128) if side == 0 else slice(cols - 128, cols)
                n = 2 * which + side
                stage_y[n, k] = part[k, :, place] + both[:, 128 * n : 128 * n + 128]
                put(stage_y.at[n, k], out.at[k, 0, :, place])
    for copy in copies:
        copy.wait()


def on_device(fields, metric_x, metric_y):
    count, _, rows, cols = fields.shape
    hbm = pl.BlockSpec(memory_space=pltpu.HBM)
    vmem = pl.BlockSpec(memory_space=pltpu.VMEM)
    block = pltpu.VMEM((count, rows, cols), F32)
    parts = pl.pallas_call(
        functools.partial(exchange, lax.axis_size("gx"), lax.axis_size("gy")),
        in_specs=[hbm] * 6,
        out_specs=[vmem] * 8,
        out_shape=[
            *[block] * 4,
            pltpu.VMEM((2, 32, cols), F32),
            pltpu.VMEM((2, 32, rows), F32),
            pltpu.VMEM((2, 32, cols), F32),
            pltpu.VMEM((2, 32, rows), F32),
        ],
        scratch_shapes=[
            pltpu.VMEM((count, rows, cols), F32),
            pltpu.VMEM((1, rows), F32),
            pltpu.VMEM((1, cols), F32),
            pltpu.VMEM((24, 128), F32),
            pltpu.VMEM((2, 2, rows, rows), BF16),
            pltpu.VMEM((2, 2, 512, 256), BF16),
            pltpu.VMEM((rows, 128), F32),
            pltpu.VMEM((5, rows, 128), F32),
            pltpu.SemaphoreType.DMA((5 + count,)),
            pltpu.SemaphoreType.DMA((4,)),
            pltpu.SemaphoreType.DMA((4,)),
        ],
        compiler_params=pltpu.CompilerParams(collective_id=0, has_side_effects=True, vmem_limit_bytes=20 << 20),
        name="exchange",
    )(
        *(
            pltpu.with_memory_space_constraint(value, pltpu.HBM)
            for value in (
                fields,
                metric_x.reshape(1, rows),
                metric_y.reshape(1, cols),
                jnp.asarray(edge_rows(128)),
                jnp.asarray(line_tables(rows)),
                jnp.asarray(window_tables()),
            )
        )
    )
    return pl.pallas_call(
        join,
        in_specs=[vmem] * 10,
        out_specs=[hbm] * 4,
        out_shape=[jax.ShapeDtypeStruct(fields.shape, F32)] * 4,
        scratch_shapes=[
            pltpu.VMEM((2, count, rows, cols), F32),
            pltpu.VMEM((4, count, rows, 128), F32),
            pltpu.SemaphoreType.DMA((8 * count,)),
        ],
        compiler_params=pltpu.CompilerParams(vmem_limit_bytes=20 << 20),
        name="join",
    )(*parts, jnp.asarray(face_tables_x(count, rows)), jnp.asarray(face_tables_y(128)))


def solution(mesh):
    whole = P(None, None, "gx", "gy")
    return jax.shard_map(
        on_device,
        mesh=mesh,
        in_specs=(whole, P("gx"), P("gy")),
        out_specs=(whole,) * 4,
        check_vma=False,
    )
```

```python
import functools

import jax
import jax.numpy as jnp
import numpy as np
from jax import lax
from jax.experimental import pallas as pl
from jax.experimental.pallas import tpu as pltpu
from jax.sharding import PartitionSpec as P

MESH = pl.DeviceIdType.MESH
F32 = jnp.float32
BF16 = jnp.bfloat16
TURN, TURN_FIRST, TURN_LAST, TURN_END, TURN_SEAM = 1, 3, 0, 2, 4
TABLES = 0

ALPHA = (1.0 / 3.0, 2.0 / 11.0)
NEAR = (7.0 / 9.0, 12.0 / 11.0 + 6.0 / 44.0)
FAR = (1.0 / 36.0, 3.0 / 44.0)
RHO = tuple(-(1.0 - np.sqrt(1.0 - 4.0 * a * a)) / (2.0 * a) for a in ALPHA)
GAIN = tuple(1.0 / np.sqrt(1.0 - 4.0 * a * a) for a in ALPHA)


def flushed(table):
    table = np.asarray(table, np.float64)
    return np.where(np.abs(table) < np.finfo(np.float32).tiny, 0.0, table)


def halves(table):
    table = flushed(table).astype(np.float32)
    high = table.astype(jnp.bfloat16)
    low = (table - high.astype(np.float32)).astype(jnp.bfloat16)
    return high, low


def green(distance, which):
    return GAIN[which] * np.power(RHO[which], np.abs(distance))


def line_tables(count):
    cells = np.arange(count)
    out = [halves(green(cells[:, None] - cells[None, :], w)) for w in range(2)]
    return np.stack([np.stack(pair) for pair in out])


def window_tables():
    rows = np.arange(512)[:, None]
    cols = np.arange(256)[None, :]
    out = [halves(green(rows - 128 - cols, w)) for w in range(2)]
    return np.stack([np.stack(pair) for pair in out])


def edge_rows(count):
    cells = np.arange(count)
    out = np.zeros((24, count))
    for w in range(2):
        out[w] = green(count - 1 - cells, w)
        out[2 + w] = green(cells, w)
        out[8 + w : 12 + w : 2] = NEAR[w]
        out[16 + w : 20 + w : 2] = FAR[w]
    return flushed(out).astype(np.float32)


def face_columns(count, which):
    cells = np.arange(count)
    out = np.zeros((count, 4))
    rho, fix = RHO[which], GAIN[which] * (RHO[which] - 1.0 / RHO[which])
    out[:, 0] = np.power(rho, cells)
    out[0, 1] = fix
    out[:, 2] = np.power(rho, count - 1 - cells)
    out[count - 1, 3] = fix
    return out


def face_tables_x(fields, count):
    tables = np.zeros((2, fields * count, 128), jnp.bfloat16)
    for w in range(2):
        high, low = halves(face_columns(count, w))
        for k in range(fields):
            for v in range(4):
                rows = slice(k * count, (k + 1) * count)
                tables[w, rows, 8 * v + k] = high[:, v]
                tables[w, rows, 32 + 8 * v + k] = low[:, v]
                tables[w, rows, 64 + 8 * v + k] = high[:, v]
    return tables


def face_tables_y(count):
    tables = np.zeros((256, 4 * count), jnp.bfloat16)
    for w in range(2):
        high, low = halves(face_columns(count, w))
        for v in range(4):
            cols = slice((2 * w + v // 2) * count, (2 * w + v // 2 + 1) * count)
            row = 32 * w + 8 * v
            tables[row, cols] = high[:, v]
            tables[64 + row, cols] = high[:, v]
            tables[128 + row, cols] = low[:, v]
    return tables


def split(value):
    high = value.astype(BF16)
    return high, (value - high.astype(F32)).astype(BF16)


def dot(a, b):
    return jnp.dot(a, b, preferred_element_type=F32)


def right_sides(f, scale, along):
    count = f.shape[along]
    place = lax.broadcasted_iota(jnp.int32, f.shape, along)
    inside = (place > 0) & (place < count - 1)
    after = pltpu.roll(f, count - 1, along)
    before = pltpu.roll(f, 1, along)
    d = jnp.where(inside, after - before, 0.0)
    e = jnp.where(inside, (after - (f + f)) + before, 0.0)
    out = []
    for which, value in ((0, d), (1, e)):
        weight = scale if which == 0 else scale * scale
        sides = pltpu.roll(value, count - 1, along) + pltpu.roll(value, 1, along)
        out.append(weight * (NEAR[which] * value + FAR[which] * sides))
    return out


def edge_weights(table, metric):
    count = metric.shape[1]
    row = lax.broadcasted_iota(jnp.int32, (8, count), 0)
    lane = lax.broadcasted_iota(jnp.int32, (8, count), 1)
    m = jnp.broadcast_to(metric, (8, count))
    base = table[0:8] * jnp.where(row % 2 == 0, m, m * m)
    out = table[8:16] * base + table[16:24] * (pltpu.roll(base, 1, 1) + pltpu.roll(base, count - 1, 1))
    out = jnp.where((lane > 0) & (lane < count - 1), out, 0.0)
    before, after = pltpu.roll(out, 1, 1), pltpu.roll(out, count - 1, 1)
    return jnp.where(row % 2 == 0, before - after, (before - out) + (after - out))


def exchange(
    nx, ny, f_hbm, mx_hbm, my_hbm, edge_hbm, tx_hbm, ty_hbm,
    ux1, ux2, uy1, uy2, sx, sy, hx, hy,
    f, mx, my, edge, tx, ty, column, load, send, recv, answer,
):
    fields, rows, cols = f.shape
    ix, iy = lax.axis_index("gx"), lax.axis_index("gy")
    peers = (
        {"gx": lax.rem(ix + 1, nx)},
        {"gx": lax.rem(ix + nx - 1, nx)},
        {"gy": lax.rem(iy + 1, ny)},
        {"gy": lax.rem(iy + ny - 1, ny)},
    )
    run = nx // 2
    place = lax.rem(ix, run)
    end, proxy, seam = place == run - 1, place == run - 2, place == 0
    inner = jnp.logical_not(end)
    right, left, up, down = peers
    barrier = pltpu.get_barrier_semaphore()

    def greet(peer):
        pl.semaphore_signal(barrier, inc=1, device_id=peer, device_id_type=MESH)

    greet(left)

    @pl.when(inner)
    def _():
        greet(up)
        greet(down)

    @pl.when(jnp.logical_not(end | proxy))
    def _():
        greet(right)

    @pl.when(end)
    def _():
        greet({**left, **up})
        greet({**left, **down})

    greeted = jnp.where(end, 1, jnp.where(proxy, 6, jnp.where(seam, 3, 4)))
    loads = [
        pltpu.make_async_copy(mx_hbm, mx, load.at[0]),
        pltpu.make_async_copy(my_hbm, my, load.at[1]),
        pltpu.make_async_copy(edge_hbm, edge, load.at[2]),
    ]
    loads += [pltpu.make_async_copy(f_hbm.at[k, 0], f.at[k], load.at[5 + k]) for k in range(fields)]
    loads += [pltpu.make_async_copy(tx_hbm, tx, load.at[3]), pltpu.make_async_copy(ty_hbm, ty, load.at[4])]
    for copy in loads[: 3 + fields]:
        copy.start()

    @pl.when(end)
    def _():
        pl.semaphore_wait(barrier, greeted)
        pl.semaphore_signal(answer.at[0], inc=1, device_id=right, device_id_type=MESH)

    for copy in loads[:3]:
        copy.wait()
    table = edge[...]
    scale_x = mx[...]
    right_block, left_block = my[:, cols - 128 : cols], my[:, 0:128]
    columns = jnp.concatenate(
        [
            edge_weights(table, scale_x)[0:4],
            edge_weights(table, right_block)[0:2],
            edge_weights(table, left_block)[2:4],
            jnp.broadcast_to(scale_x, (rows - 8, rows)),
        ],
        axis=0,
    ).T
    for n in range(9):
        column[n] = jnp.broadcast_to(columns[:, n : n + 1], (rows, 128))

    for side in range(2):
        sx[side] = jnp.zeros((32, cols), F32)
        sy[side] = jnp.zeros((32, rows), F32)
    for side, near, block in ((0, rows - 2, right_block), (1, 0, left_block)):
        for n in range(2):
            spot = slice(8 * n + 5, 8 * n + 6)
            sx[side, spot, :] = jnp.broadcast_to(scale_x[:, near + n : near + n + 1], (1, cols))
            sy[side, spot, :] = jnp.broadcast_to(block[:, near + n : near + n + 1], (1, rows))

    far1, far2 = 32, 64

    def last_face(target, k, here, value, first):
        over = value[far1:] - value[127:128]
        target[0, k : k + 1, here] = value[126:127]
        target[0, 8 + k : 9 + k, here] = value[127:128]
        target[0, 16 + k : 17 + k, here] = jnp.sum(over * column[first, far1:], axis=0, keepdims=True)
        over = over[far2 - far1 :]
        target[0, 24 + k : 25 + k, here] = jnp.sum(over * column[first + 1, far2:], axis=0, keepdims=True)

    def first_face(target, k, here, value, first):
        over = value[: 128 - far1] - value[0:1]
        target[1, k : k + 1, here] = value[0:1]
        target[1, 8 + k : 9 + k, here] = value[1:2]
        target[1, 16 + k : 17 + k, here] = jnp.sum(over * column[first, : 128 - far1], axis=0, keepdims=True)
        over = over[: 128 - far2]
        target[1, 24 + k : 25 + k, here] = jnp.sum(over * column[first + 1, : 128 - far2], axis=0, keepdims=True)

    for k in range(fields):
        loads[3 + k].wait()
        if k == TABLES:
            loads[3 + fields].start()
            loads[4 + fields].start()
        for c in range(cols // 128):
            here = slice(128 * c, 128 * c + 128)
            value = f[k, :, here]
            last_face(sx, k, here, value, 0)
            first_face(sx, k, here, value, 2)
        here = slice(0, rows)
        last_face(sy, k, here, f[k, :, cols - 128 : cols].T, 4)
        first_face(sy, k, here, f[k, :, 0:128].T, 6)

    copies = []
    for n, peer in enumerate(peers):
        source, target = (sx, hx) if n < 2 else (sy, hy)
        copies.append(
            pltpu.make_async_remote_copy(
                src_ref=source.at[n % 2],
                dst_ref=target.at[n % 2],
                send_sem=send.at[n],
                recv_sem=recv.at[n],
                device_id=peer,
                device_id_type=MESH,
            )
        )

    @pl.when(end)
    def _():
        copies[0].start()

    scale_x = jnp.concatenate([column[8]] * (cols // 128), axis=1)
    scale_y = jnp.broadcast_to(my[...], (rows, cols))

    def solve(k, carry):
        value = f[k]
        for which, (right, out) in enumerate(zip(right_sides(value, scale_x, 0), (ux1, ux2))):
            high, low = split(right)
            out[k] = dot(tx[which, 0], high) + dot(tx[which, 0], low) + dot(tx[which, 1], high)
        for which, (right, out) in enumerate(zip(right_sides(value, scale_y, 1), (uy1, uy2))):
            high, low = split(right)
            for half in range(2):
                window = slice(128 * half, 128 * half + 384)
                part = slice(128 - 128 * half, 512 - 128 * half)
                out[k, :, 256 * half : 256 * half + 256] = (
                    dot(high[:, window], ty[which, 0, part])
                    + dot(low[:, window], ty[which, 0, part])
                    + dot(high[:, window], ty[which, 1, part])
                )
        return carry

    turn = jnp.where(iy == 0, TURN_FIRST, jnp.where(iy == ny - 1, TURN_LAST, TURN))
    turn_end = jnp.where(iy == ny - 1, TURN_END - 1, TURN_END)

    def step(k, carry):
        @pl.when(inner & (k == turn))
        def _():
            pl.semaphore_wait(barrier, greeted)

            @pl.when(proxy)
            def _():
                pl.semaphore_signal(answer.at[1], inc=1, device_id=right, device_id_type=MESH)

            copies[2].start()
            copies[3].start()
            copies[0].start()

            @pl.when(jnp.logical_not(seam))
            def _():
                copies[1].start()

        @pl.when(end & (k == turn_end))
        def _():
            pl.semaphore_wait(answer.at[1], 1)
            copies[2].start()
            copies[3].start()
            copies[1].start()

        @pl.when(seam & (k == TURN_SEAM))
        def _():
            pl.semaphore_wait(answer.at[0], 1)
            copies[1].start()

        @pl.when(k == 0)
        def _():
            loads[3 + fields].wait()
            loads[4 + fields].wait()

        return solve(k, carry)

    lax.fori_loop(0, fields, step, 0)
    for copy in copies:
        copy.wait()


def face_values(own, far, side):
    near = own[1 - side]
    a, b = near[0:8], near[8:16]
    inner0, inner1 = (a, b) if side == 0 else (b, a)
    metric0, metric1 = (near[5:6], near[13:14]) if side == 0 else (near[13:14], near[5:6])
    there = far[side]
    a, b = there[0:8], there[8:16]
    outer1, outer2 = (b, a) if side == 0 else (a, b)
    beyond1, beyond2 = (there[13:14], there[5:6]) if side == 0 else (there[5:6], there[13:14])
    sign = 1.0 if side == 0 else -1.0
    differences = (
        (sign * (inner0 - outer2), sign * (inner1 - outer1)),
        ((inner0 - (outer1 + outer1)) + outer2, (inner1 - (inner0 + inner0)) + outer1),
    )
    out = []
    for which, (over, here) in enumerate(differences):
        near_by, far_by, rho, gain = NEAR[which], FAR[which], RHO[which], GAIN[which]
        m0, m1, b1, b2 = (
            (metric0, metric1, beyond1, beyond2)
            if which == 0
            else (metric0 * metric0, metric1 * metric1, beyond1 * beyond1, beyond2 * beyond2)
        )
        carry = there[16 + 8 * which : 24 + 8 * which]
        carry = carry + gain * (rho * far_by * (b2 * over) + b1 * (near_by * over + far_by * here))
        zero = m0 * (near_by * here + far_by * over)
        one = (far_by * m1) * here
        out.append((rho * carry + gain * zero + (gain / rho) * one, one))
    return out


def join(
    ux1, ux2, uy1, uy2, sx, sy, hx, hy, cx, cy,
    ox1, ox2, oy1, oy2, stage_x, stage_y, done,
):
    fields, rows, cols = ux1.shape
    middle = slice(128, cols - 128)
    copies = []

    def put(source, target):
        copy = pltpu.make_async_copy(source, target, done.at[len(copies)])
        copy.start()
        copies.append(copy)

    for part, out in ((uy1, oy1), (uy2, oy2)):
        for k in range(fields):
            put(part.at[k, :, middle], out.at[k, 0, :, middle])

    own, far = (sx[0], sx[1]), (hx[0], hx[1])
    left, right = face_values(own, far, 0), face_values(own, far, 1)
    for which, (part, out) in enumerate(((ux1, ox1), (ux2, ox2))):
        high, low = split(jnp.concatenate([*left[which], *right[which]], axis=0))
        stack = jnp.concatenate([high, high, low], axis=0)
        for k in range(fields):
            lhs = cx[which, rows * k : rows * (k + 1), 0:96]
            stage_x[which, k] = part[k] + dot(lhs, stack)
            put(stage_x.at[which, k], out.at[k, 0])

    own, far = (sy[0], sy[1]), (hy[0], hy[1])
    left, right = face_values(own, far, 0), face_values(own, far, 1)
    values = jnp.concatenate([*left[0], *right[0], *left[1], *right[1]], axis=0)
    high = values.astype(BF16).astype(F32)
    turned = jnp.concatenate([high, values - high], axis=0).T
    for k in range(fields):
        lhs = (turned if k == 0 else pltpu.roll(turned, 128 - k, 1)).astype(BF16)
        both = dot(jnp.concatenate([lhs, lhs], axis=1), cy[...])
        for which, (part, out) in enumerate(((uy1, oy1), (uy2, oy2))):
            for side in range(2):
                place = slice(0, 128) if side == 0 else slice(cols - 128, cols)
                n = 2 * which + side
                stage_y[n, k] = part[k, :, place] + both[:, 128 * n : 128 * n + 128]
                put(stage_y.at[n, k], out.at[k, 0, :, place])
    for copy in copies:
        copy.wait()


def on_device(fields, metric_x, metric_y):
    count, _, rows, cols = fields.shape
    hbm = pl.BlockSpec(memory_space=pltpu.HBM)
    vmem = pl.BlockSpec(memory_space=pltpu.VMEM)
    block = pltpu.VMEM((count, rows, cols), F32)
    parts = pl.pallas_call(
        functools.partial(exchange, lax.axis_size("gx"), lax.axis_size("gy")),
        in_specs=[hbm] * 6,
        out_specs=[vmem] * 8,
        out_shape=[
            *[block] * 4,
            pltpu.VMEM((2, 32, cols), F32),
            pltpu.VMEM((2, 32, rows), F32),
            pltpu.VMEM((2, 32, cols), F32),
            pltpu.VMEM((2, 32, rows), F32),
        ],
        scratch_shapes=[
            pltpu.VMEM((count, rows, cols), F32),
            pltpu.VMEM((1, rows), F32),
            pltpu.VMEM((1, cols), F32),
            pltpu.VMEM((24, 128), F32),
            pltpu.VMEM((2, 2, rows, rows), BF16),
            pltpu.VMEM((2, 2, 512, 256), BF16),
            pltpu.VMEM((9, rows, 128), F32),
            pltpu.SemaphoreType.DMA((5 + count,)),
            pltpu.SemaphoreType.DMA((4,)),
            pltpu.SemaphoreType.DMA((4,)),
            pltpu.SemaphoreType.REGULAR((2,)),
        ],
        compiler_params=pltpu.CompilerParams(collective_id=0, has_side_effects=True, vmem_limit_bytes=20 << 20),
        name="exchange",
    )(
        *(
            pltpu.with_memory_space_constraint(value, pltpu.HBM)
            for value in (
                fields,
                metric_x.reshape(1, rows),
                metric_y.reshape(1, cols),
                jnp.asarray(edge_rows(128)),
                jnp.asarray(line_tables(rows)),
                jnp.asarray(window_tables()),
            )
        )
    )
    return pl.pallas_call(
        join,
        in_specs=[vmem] * 10,
        out_specs=[hbm] * 4,
        out_shape=[jax.ShapeDtypeStruct(fields.shape, F32)] * 4,
        scratch_shapes=[
            pltpu.VMEM((2, count, rows, cols), F32),
            pltpu.VMEM((4, count, rows, 128), F32),
            pltpu.SemaphoreType.DMA((8 * count,)),
        ],
        compiler_params=pltpu.CompilerParams(vmem_limit_bytes=20 << 20),
        name="join",
    )(*parts, jnp.asarray(face_tables_x(count, rows)), jnp.asarray(face_tables_y(128)))


def solution(mesh):
    whole = P(None, None, "gx", "gy")
    return jax.shard_map(
        on_device,
        mesh=mesh,
        in_specs=(whole, P("gx"), P("gy")),
        out_specs=(whole,) * 4,
        check_vma=False,
    )
```

```python
import functools

import jax
import jax.numpy as jnp
import numpy as np
from jax import lax
from jax.experimental import pallas as pl
from jax.experimental.pallas import tpu as pltpu
from jax.sharding import PartitionSpec as P

MESH = pl.DeviceIdType.MESH
F32 = jnp.float32
BF16 = jnp.bfloat16
TURN, TURN_FIRST, TURN_LAST, TURN_END, TURN_SEAM, TURN_PASS = 1, 2, 0, 2, 4, 3
CHUNKS = 1
TABLES = 0

ALPHA = (1.0 / 3.0, 2.0 / 11.0)
NEAR = (7.0 / 9.0, 12.0 / 11.0 + 6.0 / 44.0)
FAR = (1.0 / 36.0, 3.0 / 44.0)
RHO = tuple(-(1.0 - np.sqrt(1.0 - 4.0 * a * a)) / (2.0 * a) for a in ALPHA)
GAIN = tuple(1.0 / np.sqrt(1.0 - 4.0 * a * a) for a in ALPHA)


def flushed(table):
    table = np.asarray(table, np.float64)
    return np.where(np.abs(table) < np.finfo(np.float32).tiny, 0.0, table)


def halves(table):
    table = flushed(table).astype(np.float32)
    high = table.astype(jnp.bfloat16)
    low = (table - high.astype(np.float32)).astype(jnp.bfloat16)
    return high, low


def green(distance, which):
    return GAIN[which] * np.power(RHO[which], np.abs(distance))


def line_tables(count):
    cells = np.arange(count)
    out = [halves(green(cells[:, None] - cells[None, :], w)) for w in range(2)]
    return np.stack([np.stack(pair) for pair in out])


def window_tables():
    rows = np.arange(512)[:, None]
    cols = np.arange(256)[None, :]
    out = [halves(green(rows - 128 - cols, w)) for w in range(2)]
    return np.stack([np.stack(pair) for pair in out])


def edge_rows(count):
    cells = np.arange(count)
    out = np.zeros((24, count))
    for w in range(2):
        out[w] = green(count - 1 - cells, w)
        out[2 + w] = green(cells, w)
        out[8 + w : 12 + w : 2] = NEAR[w]
        out[16 + w : 20 + w : 2] = FAR[w]
    return flushed(out).astype(np.float32)


def face_columns(count, which):
    cells = np.arange(count)
    out = np.zeros((count, 4))
    rho, fix = RHO[which], GAIN[which] * (RHO[which] - 1.0 / RHO[which])
    out[:, 0] = np.power(rho, cells)
    out[0, 1] = fix
    out[:, 2] = np.power(rho, count - 1 - cells)
    out[count - 1, 3] = fix
    return out


def face_tables_x(fields, count):
    tables = np.zeros((2, fields * count, 128), jnp.bfloat16)
    for w in range(2):
        high, low = halves(face_columns(count, w))
        for k in range(fields):
            for v in range(4):
                rows = slice(k * count, (k + 1) * count)
                tables[w, rows, 8 * v + k] = high[:, v]
                tables[w, rows, 32 + 8 * v + k] = low[:, v]
                tables[w, rows, 64 + 8 * v + k] = high[:, v]
    return tables


def face_tables_y(count):
    tables = np.zeros((256, 4 * count), jnp.bfloat16)
    for w in range(2):
        high, low = halves(face_columns(count, w))
        for v in range(4):
            cols = slice((2 * w + v // 2) * count, (2 * w + v // 2 + 1) * count)
            row = 32 * w + 8 * v
            tables[row, cols] = high[:, v]
            tables[64 + row, cols] = high[:, v]
            tables[128 + row, cols] = low[:, v]
    return tables


def split(value):
    high = value.astype(BF16)
    return high, (value - high.astype(F32)).astype(BF16)


def dot(a, b):
    return jnp.dot(a, b, preferred_element_type=F32)


def right_sides(f, scale, along):
    count = f.shape[along]
    place = lax.broadcasted_iota(jnp.int32, f.shape, along)
    inside = (place > 0) & (place < count - 1)
    after = pltpu.roll(f, count - 1, along)
    before = pltpu.roll(f, 1, along)
    d = jnp.where(inside, after - before, 0.0)
    e = jnp.where(inside, (after - (f + f)) + before, 0.0)
    out = []
    for which, value in ((0, d), (1, e)):
        weight = scale if which == 0 else scale * scale
        sides = pltpu.roll(value, count - 1, along) + pltpu.roll(value, 1, along)
        out.append(weight * (NEAR[which] * value + FAR[which] * sides))
    return out


def edge_weights(table, metric):
    count = metric.shape[1]
    row = lax.broadcasted_iota(jnp.int32, (8, count), 0)
    lane = lax.broadcasted_iota(jnp.int32, (8, count), 1)
    m = jnp.broadcast_to(metric, (8, count))
    base = table[0:8] * jnp.where(row % 2 == 0, m, m * m)
    out = table[8:16] * base + table[16:24] * (pltpu.roll(base, 1, 1) + pltpu.roll(base, count - 1, 1))
    out = jnp.where((lane > 0) & (lane < count - 1), out, 0.0)
    before, after = pltpu.roll(out, 1, 1), pltpu.roll(out, count - 1, 1)
    return jnp.where(row % 2 == 0, before - after, (before - out) + (after - out))


def exchange(
    nx, ny, f_hbm, mx_hbm, my_hbm, edge_hbm, tx_hbm, ty_hbm,
    ux1, ux2, uy1, uy2, sx, sy, hx, hy,
    f, mx, my, edge, tx, ty, column, load, send, recv, answer,
):
    fields, rows, cols = f.shape
    ix, iy = lax.axis_index("gx"), lax.axis_index("gy")
    peers = (
        {"gx": lax.rem(ix + 1, nx)},
        {"gx": lax.rem(ix + nx - 1, nx)},
        {"gy": lax.rem(iy + 1, ny)},
        {"gy": lax.rem(iy + ny - 1, ny)},
    )
    run = nx // 2
    place = lax.rem(ix, run)
    end, proxy, seam = place == run - 1, place == run - 2, place == 0
    inner = jnp.logical_not(end)
    even = inner & jnp.logical_not(proxy) & (lax.rem(place, 2) == 0)
    odd = inner & (lax.rem(place, 2) == 1)
    first, last = iy == 0, iy == ny - 1
    spared = even & first
    right, left, up, down = peers
    barrier = pltpu.get_barrier_semaphore()

    def greet(when, *sides):
        @pl.when(when)
        def _():
            peer = {k: v for side in sides for k, v in side.items()}
            pl.semaphore_signal(barrier, inc=1, device_id=peer, device_id_type=MESH)

    greet(ix >= 0, left)
    greet(jnp.logical_not(end | proxy), right)
    greet(inner & jnp.logical_not(even & last), up)
    greet(even & last, right, up)
    greet(inner, down)
    greet(end, left, up)
    greet(end, left, down)
    greeted = jnp.where(end, 1, jnp.where(proxy, 6, 4 - seam.astype(jnp.int32)))
    greeted = greeted - spared.astype(jnp.int32) + (odd & first).astype(jnp.int32)
    loads = [
        pltpu.make_async_copy(mx_hbm, mx, load.at[0]),
        pltpu.make_async_copy(my_hbm, my, load.at[1]),
        pltpu.make_async_copy(edge_hbm, edge, load.at[2]),
    ]
    loads += [pltpu.make_async_copy(f_hbm.at[k, 0], f.at[k], load.at[5 + k]) for k in range(fields)]
    loads += [pltpu.make_async_copy(tx_hbm, tx, load.at[3]), pltpu.make_async_copy(ty_hbm, ty, load.at[4])]
    for copy in loads[: 3 + fields]:
        copy.start()

    @pl.when(end)
    def _():
        pl.semaphore_wait(barrier, greeted)
        pl.semaphore_signal(answer.at[0], inc=1, device_id=right, device_id_type=MESH)

    for copy in loads[:3]:
        copy.wait()
    table = edge[...]
    scale_x = mx[...]
    right_block, left_block = my[:, cols - 128 : cols], my[:, 0:128]
    columns = jnp.concatenate(
        [
            edge_weights(table, scale_x)[0:4],
            edge_weights(table, right_block)[0:2],
            edge_weights(table, left_block)[2:4],
            jnp.broadcast_to(scale_x, (rows - 8, rows)),
        ],
        axis=0,
    ).T
    for n in range(9):
        column[n] = jnp.broadcast_to(columns[:, n : n + 1], (rows, 128))

    for side in range(2):
        sx[side] = jnp.zeros((32, cols), F32)
        sy[side] = jnp.zeros((32, rows), F32)
    for side, near, block in ((0, rows - 2, right_block), (1, 0, left_block)):
        for n in range(2):
            spot = slice(8 * n + 5, 8 * n + 6)
            sx[side, spot, :] = jnp.broadcast_to(scale_x[:, near + n : near + n + 1], (1, cols))
            sy[side, spot, :] = jnp.broadcast_to(block[:, near + n : near + n + 1], (1, rows))

    far1, far2 = 32, 64

    def last_face(target, k, here, value, first):
        over = value[far1:] - value[127:128]
        target[0, k : k + 1, here] = value[126:127]
        target[0, 8 + k : 9 + k, here] = value[127:128]
        target[0, 16 + k : 17 + k, here] = jnp.sum(over * column[first, far1:], axis=0, keepdims=True)
        over = over[far2 - far1 :]
        target[0, 24 + k : 25 + k, here] = jnp.sum(over * column[first + 1, far2:], axis=0, keepdims=True)

    def first_face(target, k, here, value, first):
        over = value[: 128 - far1] - value[0:1]
        target[1, k : k + 1, here] = value[0:1]
        target[1, 8 + k : 9 + k, here] = value[1:2]
        target[1, 16 + k : 17 + k, here] = jnp.sum(over * column[first, : 128 - far1], axis=0, keepdims=True)
        over = over[: 128 - far2]
        target[1, 24 + k : 25 + k, here] = jnp.sum(over * column[first + 1, : 128 - far2], axis=0, keepdims=True)

    for k in range(fields):
        loads[3 + k].wait()
        if k == TABLES:
            loads[3 + fields].start()
            loads[4 + fields].start()
        for c in range(cols // 128):
            here = slice(128 * c, 128 * c + 128)
            value = f[k, :, here]
            last_face(sx, k, here, value, 0)
            first_face(sx, k, here, value, 2)

    copies = []
    for n, peer in enumerate(peers):
        source, target, parts = (sx, hx, CHUNKS) if n < 2 else (sy, hy, 1)
        width = source.shape[2] // parts
        copies.append(
            [
                pltpu.make_async_remote_copy(
                    src_ref=source.at[n % 2, :, width * c : width * c + width],
                    dst_ref=target.at[n % 2, :, width * c : width * c + width],
                    send_sem=send.at[n, c],
                    recv_sem=recv.at[n, c],
                    device_id=peer,
                    device_id_type=MESH,
                )
                for c in range(parts)
            ]
        )

    @pl.when(end)
    def _():
        for copy in copies[0]:
            copy.start()

    for k in range(fields):
        here = slice(0, rows)
        last_face(sy, k, here, f[k, :, cols - 128 : cols].T, 4)
        first_face(sy, k, here, f[k, :, 0:128].T, 6)


    scale_x = jnp.concatenate([column[8]] * (cols // 128), axis=1)
    scale_y = jnp.broadcast_to(my[...], (rows, cols))

    def solve(k, carry):
        value = f[k]
        for which, (right, out) in enumerate(zip(right_sides(value, scale_x, 0), (ux1, ux2))):
            high, low = split(right)
            out[k] = dot(tx[which, 0], high) + dot(tx[which, 0], low) + dot(tx[which, 1], high)
        for which, (right, out) in enumerate(zip(right_sides(value, scale_y, 1), (uy1, uy2))):
            high, low = split(right)
            for half in range(2):
                window = slice(128 * half, 128 * half + 384)
                part = slice(128 - 128 * half, 512 - 128 * half)
                out[k, :, 256 * half : 256 * half + 256] = (
                    dot(high[:, window], ty[which, 0, part])
                    + dot(low[:, window], ty[which, 0, part])
                    + dot(high[:, window], ty[which, 1, part])
                )
        return carry

    heard_late = first & (odd | proxy)
    turn = jnp.where(heard_late, TURN_FIRST, jnp.where(last, TURN_LAST, TURN))
    turn_end = jnp.where(first, TURN_PASS, jnp.where(last, TURN_END - 1, TURN_END))

    def send_x(n):
        for copy in copies[n]:
            copy.start()

    def step(k, carry):
        @pl.when(inner & (k == turn))
        def _():
            pl.semaphore_wait(barrier, greeted)

            @pl.when(proxy)
            def _():
                pl.semaphore_signal(answer.at[1], inc=1, device_id=right, device_id_type=MESH)

            @pl.when(odd & first)
            def _():
                pl.semaphore_signal(answer.at[1], inc=1, device_id=left, device_id_type=MESH)

            copies[2][0].start()

            @pl.when(jnp.logical_not(spared))
            def _():
                copies[3][0].start()

            send_x(0)

            @pl.when(jnp.logical_not(seam))
            def _():
                send_x(1)

        @pl.when(end & (k == turn_end))
        def _():
            pl.semaphore_wait(answer.at[1], 1)
            copies[2][0].start()
            copies[3][0].start()
            send_x(1)

        @pl.when(spared & (k == TURN_PASS))
        def _():
            pl.semaphore_wait(answer.at[1], 1)
            copies[3][0].start()

        @pl.when(seam & (k == TURN_SEAM))
        def _():
            pl.semaphore_wait(answer.at[0], 1)
            send_x(1)

        @pl.when(k == 0)
        def _():
            loads[3 + fields].wait()
            loads[4 + fields].wait()

        return solve(k, carry)

    lax.fori_loop(0, fields, step, 0)
    for group in copies:
        for copy in group:
            copy.wait()


def face_values(own, far, side):
    near = own[1 - side]
    a, b = near[0:8], near[8:16]
    inner0, inner1 = (a, b) if side == 0 else (b, a)
    metric0, metric1 = (near[5:6], near[13:14]) if side == 0 else (near[13:14], near[5:6])
    there = far[side]
    a, b = there[0:8], there[8:16]
    outer1, outer2 = (b, a) if side == 0 else (a, b)
    beyond1, beyond2 = (there[13:14], there[5:6]) if side == 0 else (there[5:6], there[13:14])
    sign = 1.0 if side == 0 else -1.0
    differences = (
        (sign * (inner0 - outer2), sign * (inner1 - outer1)),
        ((inner0 - (outer1 + outer1)) + outer2, (inner1 - (inner0 + inner0)) + outer1),
    )
    out = []
    for which, (over, here) in enumerate(differences):
        near_by, far_by, rho, gain = NEAR[which], FAR[which], RHO[which], GAIN[which]
        m0, m1, b1, b2 = (
            (metric0, metric1, beyond1, beyond2)
            if which == 0
            else (metric0 * metric0, metric1 * metric1, beyond1 * beyond1, beyond2 * beyond2)
        )
        carry = there[16 + 8 * which : 24 + 8 * which]
        carry = carry + gain * (rho * far_by * (b2 * over) + b1 * (near_by * over + far_by * here))
        zero = m0 * (near_by * here + far_by * over)
        one = (far_by * m1) * here
        out.append((rho * carry + gain * zero + (gain / rho) * one, one))
    return out


def join(
    ux1, ux2, uy1, uy2, sx, sy, hx, hy, cx, cy,
    ox1, ox2, oy1, oy2, stage_x, stage_y, done,
):
    fields, rows, cols = ux1.shape
    middle = slice(128, cols - 128)
    copies = []

    def put(source, target):
        copy = pltpu.make_async_copy(source, target, done.at[len(copies)])
        copy.start()
        copies.append(copy)

    for part, out in ((uy1, oy1), (uy2, oy2)):
        for k in range(fields):
            put(part.at[k, :, middle], out.at[k, 0, :, middle])

    own, far = (sx[0], sx[1]), (hx[0], hx[1])
    left, right = face_values(own, far, 0), face_values(own, far, 1)
    for which, (part, out) in enumerate(((ux1, ox1), (ux2, ox2))):
        high, low = split(jnp.concatenate([*left[which], *right[which]], axis=0))
        stack = jnp.concatenate([high, high, low], axis=0)
        for k in range(fields):
            lhs = cx[which, rows * k : rows * (k + 1), 0:96]
            stage_x[which, k] = part[k] + dot(lhs, stack)
            put(stage_x.at[which, k], out.at[k, 0])

    own, far = (sy[0], sy[1]), (hy[0], hy[1])
    left, right = face_values(own, far, 0), face_values(own, far, 1)
    values = jnp.concatenate([*left[0], *right[0], *left[1], *right[1]], axis=0)
    high = values.astype(BF16).astype(F32)
    turned = jnp.concatenate([high, values - high], axis=0).T
    for k in range(fields):
        lhs = (turned if k == 0 else pltpu.roll(turned, 128 - k, 1)).astype(BF16)
        both = dot(jnp.concatenate([lhs, lhs], axis=1), cy[...])
        for which, (part, out) in enumerate(((uy1, oy1), (uy2, oy2))):
            for side in range(2):
                place = slice(0, 128) if side == 0 else slice(cols - 128, cols)
                n = 2 * which + side
                stage_y[n, k] = part[k, :, place] + both[:, 128 * n : 128 * n + 128]
                put(stage_y.at[n, k], out.at[k, 0, :, place])
    for copy in copies:
        copy.wait()


def on_device(fields, metric_x, metric_y):
    count, _, rows, cols = fields.shape
    hbm = pl.BlockSpec(memory_space=pltpu.HBM)
    vmem = pl.BlockSpec(memory_space=pltpu.VMEM)
    block = pltpu.VMEM((count, rows, cols), F32)
    parts = pl.pallas_call(
        functools.partial(exchange, lax.axis_size("gx"), lax.axis_size("gy")),
        in_specs=[hbm] * 6,
        out_specs=[vmem] * 8,
        out_shape=[
            *[block] * 4,
            pltpu.VMEM((2, 32, cols), F32),
            pltpu.VMEM((2, 32, rows), F32),
            pltpu.VMEM((2, 32, cols), F32),
            pltpu.VMEM((2, 32, rows), F32),
        ],
        scratch_shapes=[
            pltpu.VMEM((count, rows, cols), F32),
            pltpu.VMEM((1, rows), F32),
            pltpu.VMEM((1, cols), F32),
            pltpu.VMEM((24, 128), F32),
            pltpu.VMEM((2, 2, rows, rows), BF16),
            pltpu.VMEM((2, 2, 512, 256), BF16),
            pltpu.VMEM((9, rows, 128), F32),
            pltpu.SemaphoreType.DMA((5 + count,)),
            pltpu.SemaphoreType.DMA((4, CHUNKS)),
            pltpu.SemaphoreType.DMA((4, CHUNKS)),
            pltpu.SemaphoreType.REGULAR((2,)),
        ],
        compiler_params=pltpu.CompilerParams(collective_id=0, has_side_effects=True, vmem_limit_bytes=20 << 20),
        name="exchange",
    )(
        *(
            pltpu.with_memory_space_constraint(value, pltpu.HBM)
            for value in (
                fields,
                metric_x.reshape(1, rows),
                metric_y.reshape(1, cols),
                jnp.asarray(edge_rows(128)),
                jnp.asarray(line_tables(rows)),
                jnp.asarray(window_tables()),
            )
        )
    )
    return pl.pallas_call(
        join,
        in_specs=[vmem] * 10,
        out_specs=[hbm] * 4,
        out_shape=[jax.ShapeDtypeStruct(fields.shape, F32)] * 4,
        scratch_shapes=[
            pltpu.VMEM((2, count, rows, cols), F32),
            pltpu.VMEM((4, count, rows, 128), F32),
            pltpu.SemaphoreType.DMA((8 * count,)),
        ],
        compiler_params=pltpu.CompilerParams(vmem_limit_bytes=20 << 20),
        name="join",
    )(*parts, jnp.asarray(face_tables_x(count, rows)), jnp.asarray(face_tables_y(128)))


def solution(mesh):
    whole = P(None, None, "gx", "gy")
    return jax.shard_map(
        on_device,
        mesh=mesh,
        in_specs=(whole, P("gx"), P("gy")),
        out_specs=(whole,) * 4,
        check_vma=False,
    )
```

```python
import functools

import jax
import jax.numpy as jnp
import numpy as np
from jax import lax
from jax.experimental import pallas as pl
from jax.experimental.pallas import tpu as pltpu
from jax.sharding import PartitionSpec as P

MESH = pl.DeviceIdType.MESH
F32 = jnp.float32
BF16 = jnp.bfloat16
TURN, TURN_FIRST, TURN_LAST, TURN_END, TURN_SEAM, TURN_PASS = 1, 3, 0, 2, 3, 3
CHUNKS = 1
SPARE = (6, 7, 14, 15, 21)
TABLES = 0

ALPHA = (1.0 / 3.0, 2.0 / 11.0)
NEAR = (7.0 / 9.0, 12.0 / 11.0 + 6.0 / 44.0)
FAR = (1.0 / 36.0, 3.0 / 44.0)
RHO = tuple(-(1.0 - np.sqrt(1.0 - 4.0 * a * a)) / (2.0 * a) for a in ALPHA)
GAIN = tuple(1.0 / np.sqrt(1.0 - 4.0 * a * a) for a in ALPHA)


def flushed(table):
    table = np.asarray(table, np.float64)
    return np.where(np.abs(table) < np.finfo(np.float32).tiny, 0.0, table)


def halves(table):
    table = flushed(table).astype(np.float32)
    high = table.astype(jnp.bfloat16)
    low = (table - high.astype(np.float32)).astype(jnp.bfloat16)
    return high, low


def green(distance, which):
    return GAIN[which] * np.power(RHO[which], np.abs(distance))


def line_tables(count):
    cells = np.arange(count)
    out = [halves(green(cells[:, None] - cells[None, :], w)) for w in range(2)]
    return np.stack([np.concatenate([high, high, low], axis=1) for high, low in out])


def window_tables():
    rows = np.arange(512)[:, None]
    cols = np.arange(256)[None, :]
    out = [halves(green(rows - 128 - cols, w)) for w in range(2)]
    return np.stack([np.stack(pair) for pair in out])


def edge_rows(count):
    cells = np.arange(count)
    out = np.zeros((24, count))
    for w in range(2):
        out[w] = green(count - 1 - cells, w)
        out[2 + w] = green(cells, w)
        out[8 + w : 12 + w : 2] = NEAR[w]
        out[16 + w : 20 + w : 2] = FAR[w]
    return flushed(out).astype(np.float32)


def face_columns(count, which):
    cells = np.arange(count)
    out = np.zeros((count, 4))
    rho, fix = RHO[which], GAIN[which] * (RHO[which] - 1.0 / RHO[which])
    out[:, 0] = np.power(rho, cells)
    out[0, 1] = fix
    out[:, 2] = np.power(rho, count - 1 - cells)
    out[count - 1, 3] = fix
    return out


def face_tables_x(fields, count):
    tables = np.zeros((2, fields * count, 128), jnp.bfloat16)
    for w in range(2):
        high, low = halves(face_columns(count, w))
        for k in range(fields):
            for v in range(4):
                rows = slice(k * count, (k + 1) * count)
                tables[w, rows, 8 * v + k] = high[:, v]
                tables[w, rows, 32 + 8 * v + k] = low[:, v]
                tables[w, rows, 64 + 8 * v + k] = high[:, v]
    return tables


def face_tables_y(count):
    tables = np.zeros((256, 4 * count), jnp.bfloat16)
    for w in range(2):
        high, low = halves(face_columns(count, w))
        for v in range(4):
            cols = slice((2 * w + v // 2) * count, (2 * w + v // 2 + 1) * count)
            row = 32 * w + 8 * v
            tables[row, cols] = high[:, v]
            tables[64 + row, cols] = high[:, v]
            tables[128 + row, cols] = low[:, v]
    return tables


def split(value):
    high = value.astype(BF16)
    return high, (value - high.astype(F32)).astype(BF16)


def dot(a, b):
    return jnp.dot(a, b, preferred_element_type=F32)


def right_sides(f, scale, along):
    count = f.shape[along]
    place = lax.broadcasted_iota(jnp.int32, f.shape, along)
    inside = (place > 0) & (place < count - 1)
    after = pltpu.roll(f, count - 1, along)
    before = pltpu.roll(f, 1, along)
    d = jnp.where(inside, after - before, 0.0)
    e = jnp.where(inside, (after - (f + f)) + before, 0.0)
    out = []
    for which, value in ((0, d), (1, e)):
        weight = scale if which == 0 else scale * scale
        sides = pltpu.roll(value, count - 1, along) + pltpu.roll(value, 1, along)
        out.append(weight * (NEAR[which] * value + FAR[which] * sides))
    return out


def edge_weights(table, metric):
    count = metric.shape[1]
    row = lax.broadcasted_iota(jnp.int32, (8, count), 0)
    lane = lax.broadcasted_iota(jnp.int32, (8, count), 1)
    m = jnp.broadcast_to(metric, (8, count))
    base = table[0:8] * jnp.where(row % 2 == 0, m, m * m)
    out = table[8:16] * base + table[16:24] * (pltpu.roll(base, 1, 1) + pltpu.roll(base, count - 1, 1))
    out = jnp.where((lane > 0) & (lane < count - 1), out, 0.0)
    before, after = pltpu.roll(out, 1, 1), pltpu.roll(out, count - 1, 1)
    return jnp.where(row % 2 == 0, before - after, (before - out) + (after - out))


def exchange(
    nx, ny, f_hbm, mx_hbm, my_hbm, edge_hbm, tx_hbm, ty_hbm,
    ux1, ux2, uy1, uy2, sx, sy, hx, hy,
    f, mx, my, edge, tx, ty, column, load, send, recv, answer,
):
    fields, rows, cols = f.shape
    ix, iy = lax.axis_index("gx"), lax.axis_index("gy")
    peers = (
        {"gx": lax.rem(ix + 1, nx)},
        {"gx": lax.rem(ix + nx - 1, nx)},
        {"gy": lax.rem(iy + 1, ny)},
        {"gy": lax.rem(iy + ny - 1, ny)},
    )
    run = nx // 2
    place = lax.rem(ix, run)
    end, proxy, seam = place == run - 1, place == run - 2, place == 0
    inner = jnp.logical_not(end)
    even = inner & jnp.logical_not(proxy) & (lax.rem(place, 2) == 0)
    odd = inner & (lax.rem(place, 2) == 1)
    first, last = iy == 0, iy == ny - 1
    spared = even & first
    right, left, up, down = peers
    barrier = pltpu.get_barrier_semaphore()

    def greet(when, *sides):
        @pl.when(when)
        def _():
            peer = {k: v for side in sides for k, v in side.items()}
            pl.semaphore_signal(barrier, inc=1, device_id=peer, device_id_type=MESH)

    greet(ix >= 0, left)
    greet(jnp.logical_not(end | proxy), right)
    greet(inner & jnp.logical_not(even & last), up)
    greet(even & last, right, up)
    greet(inner, down)
    greet(end, left, up)
    greet(end, left, down)
    greeted = jnp.where(end, 1, jnp.where(proxy, 6, 4 - seam.astype(jnp.int32)))
    greeted = greeted - spared.astype(jnp.int32) + (odd & first).astype(jnp.int32)
    loads = [
        pltpu.make_async_copy(mx_hbm, mx, load.at[0]),
        pltpu.make_async_copy(my_hbm, my, load.at[1]),
        pltpu.make_async_copy(edge_hbm, edge, load.at[2]),
    ]
    loads += [pltpu.make_async_copy(f_hbm.at[k, 0], f.at[k], load.at[5 + k]) for k in range(fields)]
    loads += [pltpu.make_async_copy(tx_hbm, tx, load.at[3]), pltpu.make_async_copy(ty_hbm, ty, load.at[4])]
    for copy in loads[: 3 + fields]:
        copy.start()

    @pl.when(end)
    def _():
        pl.semaphore_wait(barrier, greeted)
        pl.semaphore_signal(answer.at[0], inc=1, device_id=right, device_id_type=MESH)

    for copy in loads[:3]:
        copy.wait()
    table = edge[...]
    scale_x = mx[...]
    right_block, left_block = my[:, cols - 128 : cols], my[:, 0:128]
    columns = jnp.concatenate(
        [
            edge_weights(table, scale_x)[0:4],
            edge_weights(table, right_block)[0:2],
            edge_weights(table, left_block)[2:4],
            jnp.broadcast_to(scale_x, (rows - 8, rows)),
        ],
        axis=0,
    ).T
    for n in range(9):
        column[n] = jnp.broadcast_to(columns[:, n : n + 1], (rows, 128))

    for side in range(2):
        sx[side] = jnp.zeros((24, cols), F32)
        sy[side] = jnp.zeros((24, rows), F32)
    for side, near, block in ((0, rows - 2, right_block), (1, 0, left_block)):
        for n in range(2):
            spot = slice(8 * n + 5, 8 * n + 6)
            sx[side, spot, :] = jnp.broadcast_to(scale_x[:, near + n : near + n + 1], (1, cols))
            sy[side, spot, :] = jnp.broadcast_to(block[:, near + n : near + n + 1], (1, rows))

    far1, far2 = 32, 64

    def last_face(target, k, here, value, first):
        over = value[far1:] - value[127:128]
        target[0, k : k + 1, here] = value[126:127]
        target[0, 8 + k : 9 + k, here] = value[127:128]
        target[0, 16 + k : 17 + k, here] = jnp.sum(over * column[first, far1:], axis=0, keepdims=True)
        over = over[far2 - far1 :]
        target[0, SPARE[k] : SPARE[k] + 1, here] = jnp.sum(over * column[first + 1, far2:], axis=0, keepdims=True)

    def first_face(target, k, here, value, first):
        over = value[: 128 - far1] - value[0:1]
        target[1, k : k + 1, here] = value[0:1]
        target[1, 8 + k : 9 + k, here] = value[1:2]
        target[1, 16 + k : 17 + k, here] = jnp.sum(over * column[first, : 128 - far1], axis=0, keepdims=True)
        over = over[: 128 - far2]
        target[1, SPARE[k] : SPARE[k] + 1, here] = jnp.sum(over * column[first + 1, : 128 - far2], axis=0, keepdims=True)

    for k in range(fields):
        loads[3 + k].wait()
        if k == TABLES:
            loads[3 + fields].start()
            loads[4 + fields].start()
        for c in range(cols // 128):
            here = slice(128 * c, 128 * c + 128)
            value = f[k, :, here]
            last_face(sx, k, here, value, 0)

    copies = []
    for n, peer in enumerate(peers):
        source, target, parts = (sx, hx, CHUNKS) if n < 2 else (sy, hy, 1)
        width = source.shape[2] // parts
        copies.append(
            [
                pltpu.make_async_remote_copy(
                    src_ref=source.at[n % 2, :, width * c : width * c + width],
                    dst_ref=target.at[n % 2, :, width * c : width * c + width],
                    send_sem=send.at[n, c],
                    recv_sem=recv.at[n, c],
                    device_id=peer,
                    device_id_type=MESH,
                )
                for c in range(parts)
            ]
        )

    @pl.when(end)
    def _():
        for copy in copies[0]:
            copy.start()

    for k in range(fields):
        for c in range(cols // 128):
            here = slice(128 * c, 128 * c + 128)
            first_face(sx, k, here, f[k, :, here], 2)
        here = slice(0, rows)
        last_face(sy, k, here, f[k, :, cols - 128 : cols].T, 4)
        first_face(sy, k, here, f[k, :, 0:128].T, 6)


    scale_x = jnp.concatenate([column[8]] * (cols // 128), axis=1)
    scale_y = jnp.broadcast_to(my[...], (rows, cols))

    def solve(k, carry):
        value = f[k]
        for which, (right, out) in enumerate(zip(right_sides(value, scale_x, 0), (ux1, ux2))):
            high, low = split(right)
            out[k] = dot(tx[which], jnp.concatenate([high, low, high], axis=0))
        for which, (right, out) in enumerate(zip(right_sides(value, scale_y, 1), (uy1, uy2))):
            high, low = split(right)
            for half in range(2):
                window = slice(128 * half, 128 * half + 384)
                part = slice(128 - 128 * half, 512 - 128 * half)
                out[k, :, 256 * half : 256 * half + 256] = (
                    dot(high[:, window], ty[which, 0, part])
                    + dot(low[:, window], ty[which, 0, part])
                    + dot(high[:, window], ty[which, 1, part])
                )
        return carry

    heard_late = first & (odd | proxy)
    turn = jnp.where(heard_late, TURN_FIRST, jnp.where(last, TURN_LAST, TURN))
    turn_end = jnp.where(first, TURN_PASS + 1, jnp.where(last, TURN_LAST, TURN_END))

    def send_x(n):
        for copy in copies[n]:
            copy.start()

    def step(k, carry):
        @pl.when(inner & (k == turn))
        def _():
            pl.semaphore_wait(barrier, greeted)

            @pl.when(proxy)
            def _():
                pl.semaphore_signal(answer.at[1], inc=1, device_id=right, device_id_type=MESH)

            @pl.when(odd & first)
            def _():
                pl.semaphore_signal(answer.at[1], inc=1, device_id=left, device_id_type=MESH)

            copies[2][0].start()

            @pl.when(jnp.logical_not(spared))
            def _():
                copies[3][0].start()

            send_x(0)

            @pl.when(jnp.logical_not(seam))
            def _():
                send_x(1)

        @pl.when(end & (k == turn_end))
        def _():
            pl.semaphore_wait(answer.at[1], 1)
            copies[2][0].start()
            copies[3][0].start()
            send_x(1)

        @pl.when(spared & (k == TURN_PASS))
        def _():
            pl.semaphore_wait(answer.at[1], 1)
            copies[3][0].start()

        @pl.when(seam & (k == TURN_SEAM))
        def _():
            pl.semaphore_wait(answer.at[0], 1)
            send_x(1)

        @pl.when(k == 0)
        def _():
            loads[3 + fields].wait()
            loads[4 + fields].wait()

        return solve(k, carry)

    lax.fori_loop(0, fields, step, 0)
    for group in copies:
        for copy in group:
            copy.wait()


def face_values(own, far, side):
    near = own[1 - side]
    a, b = near[0:8], near[8:16]
    inner0, inner1 = (a, b) if side == 0 else (b, a)
    metric0, metric1 = (near[5:6], near[13:14]) if side == 0 else (near[13:14], near[5:6])
    there = far[side]
    a, b = there[0:8], there[8:16]
    outer1, outer2 = (b, a) if side == 0 else (a, b)
    beyond1, beyond2 = (there[13:14], there[5:6]) if side == 0 else (there[5:6], there[13:14])
    sign = 1.0 if side == 0 else -1.0
    differences = (
        (sign * (inner0 - outer2), sign * (inner1 - outer1)),
        ((inner0 - (outer1 + outer1)) + outer2, (inner1 - (inner0 + inner0)) + outer1),
    )
    out = []
    for which, (over, here) in enumerate(differences):
        near_by, far_by, rho, gain = NEAR[which], FAR[which], RHO[which], GAIN[which]
        m0, m1, b1, b2 = (
            (metric0, metric1, beyond1, beyond2)
            if which == 0
            else (metric0 * metric0, metric1 * metric1, beyond1 * beyond1, beyond2 * beyond2)
        )
        carry = there[16:24]
        if which == 1:
            spare = [there[row : row + 1] for row in SPARE]
            carry = jnp.concatenate([*spare, jnp.zeros((3, there.shape[1]), F32)], axis=0)
        carry = carry + gain * (rho * far_by * (b2 * over) + b1 * (near_by * over + far_by * here))
        zero = m0 * (near_by * here + far_by * over)
        one = (far_by * m1) * here
        out.append((rho * carry + gain * zero + (gain / rho) * one, one))
    return out


def join(
    ux1, ux2, uy1, uy2, sx, sy, hx, hy, cx, cy,
    ox1, ox2, oy1, oy2, stage_x, stage_y, done,
):
    fields, rows, cols = ux1.shape
    middle = slice(128, cols - 128)
    copies = []

    def put(source, target):
        copy = pltpu.make_async_copy(source, target, done.at[len(copies)])
        copy.start()
        copies.append(copy)

    for part, out in ((uy1, oy1), (uy2, oy2)):
        for k in range(fields):
            put(part.at[k, :, middle], out.at[k, 0, :, middle])

    own, far = (sx[0], sx[1]), (hx[0], hx[1])
    left, right = face_values(own, far, 0), face_values(own, far, 1)
    for which, (part, out) in enumerate(((ux1, ox1), (ux2, ox2))):
        high, low = split(jnp.concatenate([*left[which], *right[which]], axis=0))
        stack = jnp.concatenate([high, high, low], axis=0)
        for k in range(fields):
            lhs = cx[which, rows * k : rows * (k + 1), 0:96]
            stage_x[which, k] = part[k] + dot(lhs, stack)
            put(stage_x.at[which, k], out.at[k, 0])

    own, far = (sy[0], sy[1]), (hy[0], hy[1])
    left, right = face_values(own, far, 0), face_values(own, far, 1)
    values = jnp.concatenate([*left[0], *right[0], *left[1], *right[1]], axis=0)
    high = values.astype(BF16).astype(F32)
    turned = jnp.concatenate([high, values - high], axis=0).T
    for k in range(fields):
        lhs = (turned if k == 0 else pltpu.roll(turned, 128 - k, 1)).astype(BF16)
        both = dot(jnp.concatenate([lhs, lhs], axis=1), cy[...])
        for which, (part, out) in enumerate(((uy1, oy1), (uy2, oy2))):
            for side in range(2):
                place = slice(0, 128) if side == 0 else slice(cols - 128, cols)
                n = 2 * which + side
                stage_y[n, k] = part[k, :, place] + both[:, 128 * n : 128 * n + 128]
                put(stage_y.at[n, k], out.at[k, 0, :, place])
    for copy in copies:
        copy.wait()


def on_device(fields, metric_x, metric_y):
    count, _, rows, cols = fields.shape
    hbm = pl.BlockSpec(memory_space=pltpu.HBM)
    vmem = pl.BlockSpec(memory_space=pltpu.VMEM)
    block = pltpu.VMEM((count, rows, cols), F32)
    parts = pl.pallas_call(
        functools.partial(exchange, lax.axis_size("gx"), lax.axis_size("gy")),
        in_specs=[hbm] * 6,
        out_specs=[vmem] * 8,
        out_shape=[
            *[block] * 4,
            pltpu.VMEM((2, 24, cols), F32),
            pltpu.VMEM((2, 24, rows), F32),
            pltpu.VMEM((2, 24, cols), F32),
            pltpu.VMEM((2, 24, rows), F32),
        ],
        scratch_shapes=[
            pltpu.VMEM((count, rows, cols), F32),
            pltpu.VMEM((1, rows), F32),
            pltpu.VMEM((1, cols), F32),
            pltpu.VMEM((24, 128), F32),
            pltpu.VMEM((2, rows, 3 * rows), BF16),
            pltpu.VMEM((2, 2, 512, 256), BF16),
            pltpu.VMEM((9, rows, 128), F32),
            pltpu.SemaphoreType.DMA((5 + count,)),
            pltpu.SemaphoreType.DMA((4, CHUNKS)),
            pltpu.SemaphoreType.DMA((4, CHUNKS)),
            pltpu.SemaphoreType.REGULAR((2,)),
        ],
        compiler_params=pltpu.CompilerParams(collective_id=0, has_side_effects=True, vmem_limit_bytes=20 << 20),
        name="exchange",
    )(
        *(
            pltpu.with_memory_space_constraint(value, pltpu.HBM)
            for value in (
                fields,
                metric_x.reshape(1, rows),
                metric_y.reshape(1, cols),
                jnp.asarray(edge_rows(128)),
                jnp.asarray(line_tables(rows)),
                jnp.asarray(window_tables()),
            )
        )
    )
    return pl.pallas_call(
        join,
        in_specs=[vmem] * 10,
        out_specs=[hbm] * 4,
        out_shape=[jax.ShapeDtypeStruct(fields.shape, F32)] * 4,
        scratch_shapes=[
            pltpu.VMEM((2, count, rows, cols), F32),
            pltpu.VMEM((4, count, rows, 128), F32),
            pltpu.SemaphoreType.DMA((8 * count,)),
        ],
        compiler_params=pltpu.CompilerParams(vmem_limit_bytes=20 << 20),
        name="join",
    )(*parts, jnp.asarray(face_tables_x(count, rows)), jnp.asarray(face_tables_y(128)))


def solution(mesh):
    whole = P(None, None, "gx", "gy")
    return jax.shard_map(
        on_device,
        mesh=mesh,
        in_specs=(whole, P("gx"), P("gy")),
        out_specs=(whole,) * 4,
        check_vma=False,
    )
```

```python
import functools

import jax
import jax.numpy as jnp
import numpy as np
from jax import lax
from jax.experimental import pallas as pl
from jax.experimental.pallas import tpu as pltpu
from jax.sharding import PartitionSpec as P

MESH = pl.DeviceIdType.MESH
F32 = jnp.float32
BF16 = jnp.bfloat16
TURN, TURN_FIRST, TURN_LAST, TURN_END, TURN_SEAM, TURN_PASS = 1, 3, 0, 2, 3, 3
CHUNKS = 1
SPARE = (6, 7, 14, 15, 21)
TABLES = 0

ALPHA = (1.0 / 3.0, 2.0 / 11.0)
NEAR = (7.0 / 9.0, 12.0 / 11.0 + 6.0 / 44.0)
FAR = (1.0 / 36.0, 3.0 / 44.0)
RHO = tuple(-(1.0 - np.sqrt(1.0 - 4.0 * a * a)) / (2.0 * a) for a in ALPHA)
GAIN = tuple(1.0 / np.sqrt(1.0 - 4.0 * a * a) for a in ALPHA)


def flushed(table):
    table = np.asarray(table, np.float64)
    return np.where(np.abs(table) < np.finfo(np.float32).tiny, 0.0, table)


def halves(table):
    table = flushed(table).astype(np.float32)
    high = table.astype(jnp.bfloat16)
    low = (table - high.astype(np.float32)).astype(jnp.bfloat16)
    return high, low


def green(distance, which):
    return GAIN[which] * np.power(RHO[which], np.abs(distance))


def line_tables(count):
    cells = np.arange(count)
    out = [halves(green(cells[:, None] - cells[None, :], w)) for w in range(2)]
    return np.stack([np.concatenate([high, high, low], axis=1) for high, low in out])


def window_tables():
    rows = np.arange(512)[:, None]
    cols = np.arange(256)[None, :]
    out = [halves(green(rows - 128 - cols, w)) for w in range(2)]
    return np.stack([np.stack(pair) for pair in out])


def edge_rows(count):
    cells = np.arange(count)
    out = np.zeros((24, count))
    for w in range(2):
        out[w] = green(count - 1 - cells, w)
        out[2 + w] = green(cells, w)
        out[8 + w : 12 + w : 2] = NEAR[w]
        out[16 + w : 20 + w : 2] = FAR[w]
    return flushed(out).astype(np.float32)


def face_columns(count, which):
    cells = np.arange(count)
    out = np.zeros((count, 4))
    rho, fix = RHO[which], GAIN[which] * (RHO[which] - 1.0 / RHO[which])
    out[:, 0] = np.power(rho, cells)
    out[0, 1] = fix
    out[:, 2] = np.power(rho, count - 1 - cells)
    out[count - 1, 3] = fix
    return out


def face_tables_x(fields, count):
    tables = np.zeros((2, fields * count, 128), jnp.bfloat16)
    for w in range(2):
        high, low = halves(face_columns(count, w))
        for k in range(fields):
            for v in range(4):
                rows = slice(k * count, (k + 1) * count)
                tables[w, rows, 8 * v + k] = high[:, v]
                tables[w, rows, 32 + 8 * v + k] = low[:, v]
                tables[w, rows, 64 + 8 * v + k] = high[:, v]
    return tables


def face_tables_y(count):
    tables = np.zeros((256, 4 * count), jnp.bfloat16)
    for w in range(2):
        high, low = halves(face_columns(count, w))
        for v in range(4):
            cols = slice((2 * w + v // 2) * count, (2 * w + v // 2 + 1) * count)
            row = 32 * w + 8 * v
            tables[row, cols] = high[:, v]
            tables[64 + row, cols] = high[:, v]
            tables[128 + row, cols] = low[:, v]
    return tables


def split(value):
    high = value.astype(BF16)
    return high, (value - high.astype(F32)).astype(BF16)


def dot(a, b):
    return jnp.dot(a, b, preferred_element_type=F32)


def right_sides(f, scale, along):
    count = f.shape[along]
    place = lax.broadcasted_iota(jnp.int32, f.shape, along)
    inside = (place > 0) & (place < count - 1)
    after = pltpu.roll(f, count - 1, along)
    before = pltpu.roll(f, 1, along)
    d = jnp.where(inside, after - before, 0.0)
    e = jnp.where(inside, (after - (f + f)) + before, 0.0)
    out = []
    for which, value in ((0, d), (1, e)):
        weight = scale if which == 0 else scale * scale
        sides = pltpu.roll(value, count - 1, along) + pltpu.roll(value, 1, along)
        out.append(weight * (NEAR[which] * value + FAR[which] * sides))
    return out


def edge_weights(table, metric):
    count = metric.shape[1]
    row = lax.broadcasted_iota(jnp.int32, (8, count), 0)
    lane = lax.broadcasted_iota(jnp.int32, (8, count), 1)
    m = jnp.broadcast_to(metric, (8, count))
    base = table[0:8] * jnp.where(row % 2 == 0, m, m * m)
    out = table[8:16] * base + table[16:24] * (pltpu.roll(base, 1, 1) + pltpu.roll(base, count - 1, 1))
    out = jnp.where((lane > 0) & (lane < count - 1), out, 0.0)
    before, after = pltpu.roll(out, 1, 1), pltpu.roll(out, count - 1, 1)
    return jnp.where(row % 2 == 0, before - after, (before - out) + (after - out))


def exchange(
    nx, ny, f_hbm, mx_hbm, my_hbm, edge_hbm, tx_hbm, ty_hbm,
    ux1, ux2, uy1, uy2, sx, sy, hx, hy,
    f, mx, my, edge, tx, ty, column, load, send, recv, answer,
):
    fields, rows, cols = f.shape
    ix, iy = lax.axis_index("gx"), lax.axis_index("gy")
    peers = (
        {"gx": lax.rem(ix + 1, nx)},
        {"gx": lax.rem(ix + nx - 1, nx)},
        {"gy": lax.rem(iy + 1, ny)},
        {"gy": lax.rem(iy + ny - 1, ny)},
    )
    run = nx // 2
    place = lax.rem(ix, run)
    end, proxy, seam = place == run - 1, place == run - 2, place == 0
    inner = jnp.logical_not(end)
    even = inner & jnp.logical_not(proxy) & (lax.rem(place, 2) == 0)
    odd = inner & (lax.rem(place, 2) == 1)
    first, last = iy == 0, iy == ny - 1
    spared = even & first
    right, left, up, down = peers
    barrier = pltpu.get_barrier_semaphore()

    def greet(when, *sides):
        @pl.when(when)
        def _():
            peer = {k: v for side in sides for k, v in side.items()}
            pl.semaphore_signal(barrier, inc=1, device_id=peer, device_id_type=MESH)

    greet(ix >= 0, left)
    greet(jnp.logical_not(end | proxy), right)
    greet(inner & jnp.logical_not(even & last), up)
    greet(even & last, right, up)
    greet(inner, down)
    greet(end, left, up)
    greet(end, left, down)
    greeted = jnp.where(end, 1, jnp.where(proxy, 6, 4 - seam.astype(jnp.int32)))
    greeted = greeted - spared.astype(jnp.int32) + (odd & first).astype(jnp.int32)
    loads = [
        pltpu.make_async_copy(mx_hbm, mx, load.at[0]),
        pltpu.make_async_copy(my_hbm, my, load.at[1]),
        pltpu.make_async_copy(edge_hbm, edge, load.at[2]),
    ]
    loads += [pltpu.make_async_copy(f_hbm.at[k, 0], f.at[k], load.at[5 + k]) for k in range(fields)]
    loads += [pltpu.make_async_copy(tx_hbm, tx, load.at[3]), pltpu.make_async_copy(ty_hbm, ty, load.at[4])]
    for copy in loads[: 3 + fields]:
        copy.start()

    @pl.when(end)
    def _():
        pl.semaphore_wait(barrier, greeted)
        pl.semaphore_signal(answer.at[0], inc=1, device_id=right, device_id_type=MESH)

    for copy in loads[:3]:
        copy.wait()
    table = edge[...]
    scale_x = mx[...]
    right_block, left_block = my[:, cols - 128 : cols], my[:, 0:128]
    columns = jnp.concatenate(
        [
            edge_weights(table, scale_x)[0:4],
            edge_weights(table, right_block)[0:2],
            edge_weights(table, left_block)[2:4],
            jnp.broadcast_to(scale_x, (rows - 8, rows)),
        ],
        axis=0,
    ).T
    for n in range(9):
        column[n] = jnp.broadcast_to(columns[:, n : n + 1], (rows, 128))

    for side in range(2):
        sx[side] = jnp.zeros((24, cols), F32)
        sy[side] = jnp.zeros((24, rows), F32)
    for side, near, block in ((0, rows - 2, right_block), (1, 0, left_block)):
        for n in range(2):
            spot = slice(8 * n + 5, 8 * n + 6)
            sx[side, spot, :] = jnp.broadcast_to(scale_x[:, near + n : near + n + 1], (1, cols))
            sy[side, spot, :] = jnp.broadcast_to(block[:, near + n : near + n + 1], (1, rows))

    far1, far2 = 32, 64

    def last_face(target, k, here, value, first):
        over = value[far1:] - value[127:128]
        target[0, k : k + 1, here] = value[126:127]
        target[0, 8 + k : 9 + k, here] = value[127:128]
        target[0, 16 + k : 17 + k, here] = jnp.sum(over * column[first, far1:], axis=0, keepdims=True)
        over = over[far2 - far1 :]
        target[0, SPARE[k] : SPARE[k] + 1, here] = jnp.sum(over * column[first + 1, far2:], axis=0, keepdims=True)

    def first_face(target, k, here, value, first):
        over = value[: 128 - far1] - value[0:1]
        target[1, k : k + 1, here] = value[0:1]
        target[1, 8 + k : 9 + k, here] = value[1:2]
        target[1, 16 + k : 17 + k, here] = jnp.sum(over * column[first, : 128 - far1], axis=0, keepdims=True)
        over = over[: 128 - far2]
        target[1, SPARE[k] : SPARE[k] + 1, here] = jnp.sum(over * column[first + 1, : 128 - far2], axis=0, keepdims=True)

    for k in range(fields):
        loads[3 + k].wait()
        if k == TABLES:
            loads[3 + fields].start()
            loads[4 + fields].start()
        for c in range(cols // 128):
            here = slice(128 * c, 128 * c + 128)
            value = f[k, :, here]
            last_face(sx, k, here, value, 0)

    copies = []
    for n, peer in enumerate(peers):
        source, target, parts = (sx, hx, CHUNKS) if n < 2 else (sy, hy, 1)
        width = source.shape[2] // parts
        copies.append(
            [
                pltpu.make_async_remote_copy(
                    src_ref=source.at[n % 2, :, width * c : width * c + width],
                    dst_ref=target.at[n % 2, :, width * c : width * c + width],
                    send_sem=send.at[n, c],
                    recv_sem=recv.at[n, c],
                    device_id=peer,
                    device_id_type=MESH,
                )
                for c in range(parts)
            ]
        )

    @pl.when(end)
    def _():
        for copy in copies[0]:
            copy.start()

    for k in range(fields):
        for c in range(cols // 128):
            here = slice(128 * c, 128 * c + 128)
            first_face(sx, k, here, f[k, :, here], 2)
        here = slice(0, rows)
        last_face(sy, k, here, f[k, :, cols - 128 : cols].T, 4)
        first_face(sy, k, here, f[k, :, 0:128].T, 6)


    scale_x = jnp.concatenate([column[8]] * (cols // 128), axis=1)
    scale_y = jnp.broadcast_to(my[...], (rows, cols))

    def solve(k, carry):
        value = f[k]
        for which, (right, out) in enumerate(zip(right_sides(value, scale_x, 0), (ux1, ux2))):
            high, low = split(right)
            out[k] = dot(tx[which], jnp.concatenate([high, low, high], axis=0))
        for which, (right, out) in enumerate(zip(right_sides(value, scale_y, 1), (uy1, uy2))):
            high, low = split(right)
            for half in range(2):
                window = slice(128 * half, 128 * half + 384)
                part = slice(128 - 128 * half, 512 - 128 * half)
                out[k, :, 256 * half : 256 * half + 256] = (
                    dot(high[:, window], ty[which, 0, part])
                    + dot(low[:, window], ty[which, 0, part])
                    + dot(high[:, window], ty[which, 1, part])
                )
        return carry

    heard_late = first & (odd | proxy)
    turn = jnp.where(heard_late, TURN_FIRST, jnp.where(last, TURN_LAST, TURN))
    turn_end = jnp.where(first, TURN_PASS + 1, jnp.where(last, TURN_LAST, TURN_END))

    def send_x(n):
        for copy in copies[n]:
            copy.start()

    def step(k, carry):
        @pl.when(inner & (k == turn))
        def _():
            pl.semaphore_wait(barrier, greeted)

            @pl.when(proxy)
            def _():
                pl.semaphore_signal(answer.at[1], inc=1, device_id=right, device_id_type=MESH)

            @pl.when(odd & first)
            def _():
                pl.semaphore_signal(answer.at[1], inc=1, device_id=left, device_id_type=MESH)

            copies[2][0].start()

            @pl.when(jnp.logical_not(spared))
            def _():
                copies[3][0].start()

            send_x(0)

            @pl.when(jnp.logical_not(seam))
            def _():
                send_x(1)

        @pl.when(end & (k == turn_end))
        def _():
            pl.semaphore_wait(answer.at[1], 1)
            copies[2][0].start()
            copies[3][0].start()
            send_x(1)

        @pl.when(spared & (k == TURN_PASS))
        def _():
            pl.semaphore_wait(answer.at[1], 1)
            copies[3][0].start()

        @pl.when(seam & (k == TURN_SEAM))
        def _():
            pl.semaphore_wait(answer.at[0], 1)
            send_x(1)

        @pl.when(k == 0)
        def _():
            loads[3 + fields].wait()
            loads[4 + fields].wait()

        return solve(k, carry)

    lax.fori_loop(0, fields, step, 0)
    for group in copies:
        for copy in group:
            copy.wait()


def face_values(own, far, side):
    near = own[1 - side]
    a, b = near[0:8], near[8:16]
    inner0, inner1 = (a, b) if side == 0 else (b, a)
    metric0, metric1 = (near[5:6], near[13:14]) if side == 0 else (near[13:14], near[5:6])
    there = far[side]
    a, b = there[0:8], there[8:16]
    outer1, outer2 = (b, a) if side == 0 else (a, b)
    beyond1, beyond2 = (there[13:14], there[5:6]) if side == 0 else (there[5:6], there[13:14])
    sign = 1.0 if side == 0 else -1.0
    differences = (
        (sign * (inner0 - outer2), sign * (inner1 - outer1)),
        ((inner0 - (outer1 + outer1)) + outer2, (inner1 - (inner0 + inner0)) + outer1),
    )
    out = []
    for which, (over, here) in enumerate(differences):
        near_by, far_by, rho, gain = NEAR[which], FAR[which], RHO[which], GAIN[which]
        m0, m1, b1, b2 = (
            (metric0, metric1, beyond1, beyond2)
            if which == 0
            else (metric0 * metric0, metric1 * metric1, beyond1 * beyond1, beyond2 * beyond2)
        )
        carry = there[16:24]
        if which == 1:
            spare = [there[row : row + 1] for row in SPARE]
            carry = jnp.concatenate([*spare, jnp.zeros((3, there.shape[1]), F32)], axis=0)
        carry = carry + gain * (rho * far_by * (b2 * over) + b1 * (near_by * over + far_by * here))
        zero = m0 * (near_by * here + far_by * over)
        one = (far_by * m1) * here
        out.append((rho * carry + gain * zero + (gain / rho) * one, one))
    return out


def join(
    ux1, ux2, uy1, uy2, sx, sy, hx, hy, cx, cy,
    ox1, ox2, oy1, oy2, stage_x, stage_y, done,
):
    fields, rows, cols = ux1.shape
    middle = slice(128, cols - 128)

    def put(source, target, n):
        pltpu.make_async_copy(source, target, done.at[n]).start()

    for n, (part, out) in enumerate(((uy1, oy1), (uy2, oy2))):
        for k in range(fields):
            put(part.at[k, :, middle], out.at[k, 0, :, middle], 2 + n)

    own, far = (sx[0], sx[1]), (hx[0], hx[1])
    left, right = face_values(own, far, 0), face_values(own, far, 1)
    for which, (part, out) in enumerate(((ux1, ox1), (ux2, ox2))):
        high, low = split(jnp.concatenate([*left[which], *right[which]], axis=0))
        stack = jnp.concatenate([high, high, low], axis=0)
        for k in range(fields):
            lhs = cx[which, rows * k : rows * (k + 1), 0:96]
            stage_x[which, k] = part[k] + dot(lhs, stack)
            put(stage_x.at[which, k], out.at[k, 0], which)

    own, far = (sy[0], sy[1]), (hy[0], hy[1])
    left, right = face_values(own, far, 0), face_values(own, far, 1)
    values = jnp.concatenate([*left[0], *right[0], *left[1], *right[1]], axis=0)
    high = values.astype(BF16).astype(F32)
    turned = jnp.concatenate([high, values - high], axis=0).T
    for k in range(fields):
        lhs = (turned if k == 0 else pltpu.roll(turned, 128 - k, 1)).astype(BF16)
        both = dot(jnp.concatenate([lhs, lhs], axis=1), cy[...])
        for which, (part, out) in enumerate(((uy1, oy1), (uy2, oy2))):
            for side in range(2):
                place = slice(0, 128) if side == 0 else slice(cols - 128, cols)
                n = 2 * which + side
                stage_y[n, k] = part[k, :, place] + both[:, 128 * n : 128 * n + 128]
                put(stage_y.at[n, k], out.at[k, 0, :, place], 2 + which)
    for n, (part, out) in enumerate(((ux1, ox1), (ux2, ox2), (uy1, oy1), (uy2, oy2))):
        pltpu.make_async_copy(part, out.at[:, 0], done.at[n]).wait()


def on_device(fields, metric_x, metric_y):
    count, _, rows, cols = fields.shape
    hbm = pl.BlockSpec(memory_space=pltpu.HBM)
    vmem = pl.BlockSpec(memory_space=pltpu.VMEM)
    block = pltpu.VMEM((count, rows, cols), F32)
    parts = pl.pallas_call(
        functools.partial(exchange, lax.axis_size("gx"), lax.axis_size("gy")),
        in_specs=[hbm] * 6,
        out_specs=[vmem] * 8,
        out_shape=[
            *[block] * 4,
            pltpu.VMEM((2, 24, cols), F32),
            pltpu.VMEM((2, 24, rows), F32),
            pltpu.VMEM((2, 24, cols), F32),
            pltpu.VMEM((2, 24, rows), F32),
        ],
        scratch_shapes=[
            pltpu.VMEM((count, rows, cols), F32),
            pltpu.VMEM((1, rows), F32),
            pltpu.VMEM((1, cols), F32),
            pltpu.VMEM((24, 128), F32),
            pltpu.VMEM((2, rows, 3 * rows), BF16),
            pltpu.VMEM((2, 2, 512, 256), BF16),
            pltpu.VMEM((9, rows, 128), F32),
            pltpu.SemaphoreType.DMA((5 + count,)),
            pltpu.SemaphoreType.DMA((4, CHUNKS)),
            pltpu.SemaphoreType.DMA((4, CHUNKS)),
            pltpu.SemaphoreType.REGULAR((2,)),
        ],
        compiler_params=pltpu.CompilerParams(collective_id=0, has_side_effects=True, vmem_limit_bytes=20 << 20),
        name="exchange",
    )(
        *(
            pltpu.with_memory_space_constraint(value, pltpu.HBM)
            for value in (
                fields,
                metric_x.reshape(1, rows),
                metric_y.reshape(1, cols),
                jnp.asarray(edge_rows(128)),
                jnp.asarray(line_tables(rows)),
                jnp.asarray(window_tables()),
            )
        )
    )
    return pl.pallas_call(
        join,
        in_specs=[vmem] * 10,
        out_specs=[hbm] * 4,
        out_shape=[jax.ShapeDtypeStruct(fields.shape, F32)] * 4,
        scratch_shapes=[
            pltpu.VMEM((2, count, rows, cols), F32),
            pltpu.VMEM((4, count, rows, 128), F32),
            pltpu.SemaphoreType.DMA((4,)),
        ],
        compiler_params=pltpu.CompilerParams(vmem_limit_bytes=20 << 20),
        name="join",
    )(*parts, jnp.asarray(face_tables_x(count, rows)), jnp.asarray(face_tables_y(128)))


def solution(mesh):
    whole = P(None, None, "gx", "gy")
    return jax.shard_map(
        on_device,
        mesh=mesh,
        in_specs=(whole, P("gx"), P("gy")),
        out_specs=(whole,) * 4,
        check_vma=False,
    )
```

```python
import functools

import jax
import jax.numpy as jnp
import numpy as np
from jax import lax
from jax.experimental import pallas as pl
from jax.experimental.pallas import tpu as pltpu
from jax.sharding import PartitionSpec as P

MESH = pl.DeviceIdType.MESH
F32 = jnp.float32
BF16 = jnp.bfloat16
TURN, TURN_FIRST, TURN_LAST, TURN_END, TURN_SEAM, TURN_PASS = 1, 3, 0, 2, 3, 3
CHUNKS = 1
SPARE = (6, 7, 14, 15, 21)
TABLES = 0

ALPHA = (1.0 / 3.0, 2.0 / 11.0)
NEAR = (7.0 / 9.0, 12.0 / 11.0 + 6.0 / 44.0)
FAR = (1.0 / 36.0, 3.0 / 44.0)
RHO = tuple(-(1.0 - np.sqrt(1.0 - 4.0 * a * a)) / (2.0 * a) for a in ALPHA)
GAIN = tuple(1.0 / np.sqrt(1.0 - 4.0 * a * a) for a in ALPHA)


def flushed(table):
    table = np.asarray(table, np.float64)
    return np.where(np.abs(table) < np.finfo(np.float32).tiny, 0.0, table)


def halves(table):
    table = flushed(table).astype(np.float32)
    high = table.astype(jnp.bfloat16)
    low = (table - high.astype(np.float32)).astype(jnp.bfloat16)
    return high, low


def green(distance, which):
    return GAIN[which] * np.power(RHO[which], np.abs(distance))


def line_tables(count):
    cells = np.arange(count)
    out = [halves(green(cells[:, None] - cells[None, :], w)) for w in range(2)]
    return np.stack([np.concatenate([high, high, low], axis=1) for high, low in out])


def window_tables():
    rows = np.arange(512)[:, None]
    cols = np.arange(256)[None, :]
    out = [halves(green(rows - 128 - cols, w)) for w in range(2)]
    return np.stack([np.stack(pair) for pair in out])


def edge_rows(count):
    cells = np.arange(count)
    out = np.zeros((24, count))
    for w in range(2):
        out[w] = green(count - 1 - cells, w)
        out[2 + w] = green(cells, w)
        out[8 + w : 12 + w : 2] = NEAR[w]
        out[16 + w : 20 + w : 2] = FAR[w]
    return flushed(out).astype(np.float32)


def face_columns(count, which):
    cells = np.arange(count)
    out = np.zeros((count, 4))
    rho, fix = RHO[which], GAIN[which] * (RHO[which] - 1.0 / RHO[which])
    out[:, 0] = np.power(rho, cells)
    out[0, 1] = fix
    out[:, 2] = np.power(rho, count - 1 - cells)
    out[count - 1, 3] = fix
    return out


def face_tables_x(fields, count):
    tables = np.zeros((2, fields * count, 128), jnp.bfloat16)
    for w in range(2):
        high, low = halves(face_columns(count, w))
        for k in range(fields):
            for v in range(4):
                rows = slice(k * count, (k + 1) * count)
                tables[w, rows, 8 * v + k] = high[:, v]
                tables[w, rows, 32 + 8 * v + k] = low[:, v]
                tables[w, rows, 64 + 8 * v + k] = high[:, v]
    return tables


def face_tables_y(count):
    tables = np.zeros((256, 4 * count), jnp.bfloat16)
    for w in range(2):
        high, low = halves(face_columns(count, w))
        for v in range(4):
            cols = slice((2 * w + v // 2) * count, (2 * w + v // 2 + 1) * count)
            row = 32 * w + 8 * v
            tables[row, cols] = high[:, v]
            tables[64 + row, cols] = high[:, v]
            tables[128 + row, cols] = low[:, v]
    return tables


def split(value):
    high = value.astype(BF16)
    return high, (value - high.astype(F32)).astype(BF16)


def dot(a, b):
    return jnp.dot(a, b, preferred_element_type=F32)


def right_sides(f, scale, along):
    count = f.shape[along]
    place = lax.broadcasted_iota(jnp.int32, f.shape, along)
    inside = (place > 0) & (place < count - 1)
    after = pltpu.roll(f, count - 1, along)
    before = pltpu.roll(f, 1, along)
    d = jnp.where(inside, after - before, 0.0)
    e = jnp.where(inside, (after - (f + f)) + before, 0.0)
    out = []
    for which, value in ((0, d), (1, e)):
        weight = scale if which == 0 else scale * scale
        sides = pltpu.roll(value, count - 1, along) + pltpu.roll(value, 1, along)
        out.append(weight * (NEAR[which] * value + FAR[which] * sides))
    return out


def edge_weights(table, metric):
    count = metric.shape[1]
    row = lax.broadcasted_iota(jnp.int32, (8, count), 0)
    lane = lax.broadcasted_iota(jnp.int32, (8, count), 1)
    m = jnp.broadcast_to(metric, (8, count))
    base = table[0:8] * jnp.where(row % 2 == 0, m, m * m)
    out = table[8:16] * base + table[16:24] * (pltpu.roll(base, 1, 1) + pltpu.roll(base, count - 1, 1))
    out = jnp.where((lane > 0) & (lane < count - 1), out, 0.0)
    before, after = pltpu.roll(out, 1, 1), pltpu.roll(out, count - 1, 1)
    return jnp.where(row % 2 == 0, before - after, (before - out) + (after - out))


def exchange(
    nx, ny, f_hbm, mx_hbm, my_hbm, edge_hbm, tx_hbm, ty_hbm,
    ux1, ux2, uy1, uy2, sx, sy, hx, hy,
    f, mx, my, edge, tx, ty, column, load, send, recv, answer,
):
    fields, rows, cols = f.shape
    loads = [
        pltpu.make_async_copy(mx_hbm, mx, load.at[0]),
        pltpu.make_async_copy(my_hbm, my, load.at[1]),
        pltpu.make_async_copy(edge_hbm, edge, load.at[2]),
    ]
    loads += [pltpu.make_async_copy(f_hbm.at[k, 0], f.at[k], load.at[5 + k]) for k in range(fields)]
    loads += [pltpu.make_async_copy(tx_hbm, tx, load.at[3]), pltpu.make_async_copy(ty_hbm, ty, load.at[4])]
    for copy in loads[: 3 + fields]:
        copy.start()

    ix, iy = lax.axis_index("gx"), lax.axis_index("gy")
    peers = (
        {"gx": lax.rem(ix + 1, nx)},
        {"gx": lax.rem(ix + nx - 1, nx)},
        {"gy": lax.rem(iy + 1, ny)},
        {"gy": lax.rem(iy + ny - 1, ny)},
    )
    run = nx // 2
    place = lax.rem(ix, run)
    end, proxy, seam = place == run - 1, place == run - 2, place == 0
    inner = jnp.logical_not(end)
    even = inner & jnp.logical_not(proxy) & (lax.rem(place, 2) == 0)
    odd = inner & (lax.rem(place, 2) == 1)
    first, last = iy == 0, iy == ny - 1
    spared = even & first
    right, left, up, down = peers
    barrier = pltpu.get_barrier_semaphore()

    def greet(when, *sides):
        @pl.when(when)
        def _():
            peer = {k: v for side in sides for k, v in side.items()}
            pl.semaphore_signal(barrier, inc=1, device_id=peer, device_id_type=MESH)

    greet(ix >= 0, left)
    greet(jnp.logical_not(end | proxy), right)
    greet(inner & jnp.logical_not(even & last), up)
    greet(even & last, right, up)
    greet(inner, down)
    greet(end, left, up)
    greet(end, left, down)
    greeted = jnp.where(end, 1, jnp.where(proxy, 6, 4 - seam.astype(jnp.int32)))
    greeted = greeted - spared.astype(jnp.int32) + (odd & first).astype(jnp.int32)
    @pl.when(end)
    def _():
        pl.semaphore_wait(barrier, greeted)
        pl.semaphore_signal(answer.at[0], inc=1, device_id=right, device_id_type=MESH)

    for copy in loads[:3]:
        copy.wait()
    table = edge[...]
    scale_x = mx[...]
    right_block, left_block = my[:, cols - 128 : cols], my[:, 0:128]
    columns = jnp.concatenate(
        [
            edge_weights(table, scale_x)[0:4],
            edge_weights(table, right_block)[0:2],
            edge_weights(table, left_block)[2:4],
            jnp.broadcast_to(scale_x, (rows - 8, rows)),
        ],
        axis=0,
    ).T
    for n in range(9):
        column[n] = jnp.broadcast_to(columns[:, n : n + 1], (rows, 128))

    for side in range(2):
        sx[side] = jnp.zeros((24, cols), F32)
        sy[side] = jnp.zeros((24, rows), F32)
    for side, near, block in ((0, rows - 2, right_block), (1, 0, left_block)):
        for n in range(2):
            spot = slice(8 * n + 5, 8 * n + 6)
            sx[side, spot, :] = jnp.broadcast_to(scale_x[:, near + n : near + n + 1], (1, cols))
            sy[side, spot, :] = jnp.broadcast_to(block[:, near + n : near + n + 1], (1, rows))

    far1, far2 = 32, 64

    def last_face(target, k, here, value, first):
        over = value[far1:] - value[127:128]
        target[0, k : k + 1, here] = value[126:127]
        target[0, 8 + k : 9 + k, here] = value[127:128]
        target[0, 16 + k : 17 + k, here] = jnp.sum(over * column[first, far1:], axis=0, keepdims=True)
        over = over[far2 - far1 :]
        target[0, SPARE[k] : SPARE[k] + 1, here] = jnp.sum(over * column[first + 1, far2:], axis=0, keepdims=True)

    def first_face(target, k, here, value, first):
        over = value[: 128 - far1] - value[0:1]
        target[1, k : k + 1, here] = value[0:1]
        target[1, 8 + k : 9 + k, here] = value[1:2]
        target[1, 16 + k : 17 + k, here] = jnp.sum(over * column[first, : 128 - far1], axis=0, keepdims=True)
        over = over[: 128 - far2]
        target[1, SPARE[k] : SPARE[k] + 1, here] = jnp.sum(over * column[first + 1, : 128 - far2], axis=0, keepdims=True)

    for k in range(fields):
        loads[3 + k].wait()
        if k == TABLES:
            loads[3 + fields].start()
            loads[4 + fields].start()
        for c in range(cols // 128):
            here = slice(128 * c, 128 * c + 128)
            value = f[k, :, here]
            last_face(sx, k, here, value, 0)

    copies = []
    for n, peer in enumerate(peers):
        source, target, parts = (sx, hx, CHUNKS) if n < 2 else (sy, hy, 1)
        width = source.shape[2] // parts
        copies.append(
            [
                pltpu.make_async_remote_copy(
                    src_ref=source.at[n % 2, :, width * c : width * c + width],
                    dst_ref=target.at[n % 2, :, width * c : width * c + width],
                    send_sem=send.at[n, c],
                    recv_sem=recv.at[n, c],
                    device_id=peer,
                    device_id_type=MESH,
                )
                for c in range(parts)
            ]
        )

    @pl.when(end)
    def _():
        for copy in copies[0]:
            copy.start()

    for k in range(fields):
        for c in range(cols // 128):
            here = slice(128 * c, 128 * c + 128)
            first_face(sx, k, here, f[k, :, here], 2)
        here = slice(0, rows)
        last_face(sy, k, here, f[k, :, cols - 128 : cols].T, 4)
        first_face(sy, k, here, f[k, :, 0:128].T, 6)


    scale_x = jnp.concatenate([column[8]] * (cols // 128), axis=1)
    scale_y = jnp.broadcast_to(my[...], (rows, cols))

    def solve(k, carry):
        value = f[k]
        for which, (right, out) in enumerate(zip(right_sides(value, scale_x, 0), (ux1, ux2))):
            high, low = split(right)
            out[k] = dot(tx[which], jnp.concatenate([high, low, high], axis=0))
        for which, (right, out) in enumerate(zip(right_sides(value, scale_y, 1), (uy1, uy2))):
            high, low = split(right)
            for half in range(2):
                window = slice(128 * half, 128 * half + 384)
                part = slice(128 - 128 * half, 512 - 128 * half)
                out[k, :, 256 * half : 256 * half + 256] = (
                    dot(high[:, window], ty[which, 0, part])
                    + dot(low[:, window], ty[which, 0, part])
                    + dot(high[:, window], ty[which, 1, part])
                )
        return carry

    heard_late = first & (odd | proxy)
    turn = jnp.where(heard_late, TURN_FIRST, jnp.where(last, TURN_LAST, TURN))
    turn_end = jnp.where(first, TURN_PASS + 1, jnp.where(last, TURN_LAST, TURN_END))

    def send_x(n):
        for copy in copies[n]:
            copy.start()

    def step(k, carry):
        @pl.when(inner & (k == turn))
        def _():
            pl.semaphore_wait(barrier, greeted)

            @pl.when(proxy)
            def _():
                pl.semaphore_signal(answer.at[1], inc=1, device_id=right, device_id_type=MESH)

            @pl.when(odd & first)
            def _():
                pl.semaphore_signal(answer.at[1], inc=1, device_id=left, device_id_type=MESH)

            copies[2][0].start()

            @pl.when(jnp.logical_not(spared))
            def _():
                copies[3][0].start()

            send_x(0)

            @pl.when(jnp.logical_not(seam))
            def _():
                send_x(1)

        @pl.when(end & (k == turn_end))
        def _():
            pl.semaphore_wait(answer.at[1], 1)
            copies[2][0].start()
            copies[3][0].start()
            send_x(1)

        @pl.when(spared & (k == TURN_PASS))
        def _():
            pl.semaphore_wait(answer.at[1], 1)
            copies[3][0].start()

        @pl.when(seam & (k == TURN_SEAM))
        def _():
            pl.semaphore_wait(answer.at[0], 1)
            send_x(1)

        @pl.when(k == 0)
        def _():
            loads[3 + fields].wait()
            loads[4 + fields].wait()

        return solve(k, carry)

    lax.fori_loop(0, fields, step, 0)
    for group in copies:
        for copy in group:
            copy.wait()


def face_values(own, far, side):
    near = own[1 - side]
    a, b = near[0:8], near[8:16]
    inner0, inner1 = (a, b) if side == 0 else (b, a)
    metric0, metric1 = (near[5:6], near[13:14]) if side == 0 else (near[13:14], near[5:6])
    there = far[side]
    a, b = there[0:8], there[8:16]
    outer1, outer2 = (b, a) if side == 0 else (a, b)
    beyond1, beyond2 = (there[13:14], there[5:6]) if side == 0 else (there[5:6], there[13:14])
    sign = 1.0 if side == 0 else -1.0
    differences = (
        (sign * (inner0 - outer2), sign * (inner1 - outer1)),
        ((inner0 - (outer1 + outer1)) + outer2, (inner1 - (inner0 + inner0)) + outer1),
    )
    out = []
    for which, (over, here) in enumerate(differences):
        near_by, far_by, rho, gain = NEAR[which], FAR[which], RHO[which], GAIN[which]
        m0, m1, b1, b2 = (
            (metric0, metric1, beyond1, beyond2)
            if which == 0
            else (metric0 * metric0, metric1 * metric1, beyond1 * beyond1, beyond2 * beyond2)
        )
        carry = there[16:24]
        if which == 1:
            spare = [there[row : row + 1] for row in SPARE]
            carry = jnp.concatenate([*spare, jnp.zeros((3, there.shape[1]), F32)], axis=0)
        carry = carry + gain * (rho * far_by * (b2 * over) + b1 * (near_by * over + far_by * here))
        zero = m0 * (near_by * here + far_by * over)
        one = (far_by * m1) * here
        out.append((rho * carry + gain * zero + (gain / rho) * one, one))
    return out


def join(
    ux1, ux2, uy1, uy2, sx, sy, hx, hy, cx, cy,
    ox1, ox2, oy1, oy2, stage_x, stage_y, done,
):
    fields, rows, cols = ux1.shape
    middle = slice(128, cols - 128)

    def put(source, target, n):
        pltpu.make_async_copy(source, target, done.at[n]).start()

    for n, (part, out) in enumerate(((uy1, oy1), (uy2, oy2))):
        for k in range(fields):
            put(part.at[k, :, middle], out.at[k, 0, :, middle], 2 + n)

    own, far = (sx[0], sx[1]), (hx[0], hx[1])
    left, right = face_values(own, far, 0), face_values(own, far, 1)
    for which, (part, out) in enumerate(((ux1, ox1), (ux2, ox2))):
        high, low = split(jnp.concatenate([*left[which], *right[which]], axis=0))
        stack = jnp.concatenate([high, high, low], axis=0)
        for k in range(fields):
            lhs = cx[which, rows * k : rows * (k + 1), 0:96]
            stage_x[which, k] = part[k] + dot(lhs, stack)
            put(stage_x.at[which, k], out.at[k, 0], which)

    own, far = (sy[0], sy[1]), (hy[0], hy[1])
    left, right = face_values(own, far, 0), face_values(own, far, 1)
    values = jnp.concatenate([*left[0], *right[0], *left[1], *right[1]], axis=0)
    high = values.astype(BF16).astype(F32)
    turned = jnp.concatenate([high, values - high], axis=0).T
    for k in range(fields):
        lhs = (turned if k == 0 else pltpu.roll(turned, 128 - k, 1)).astype(BF16)
        both = dot(jnp.concatenate([lhs, lhs], axis=1), cy[...])
        for which, (part, out) in enumerate(((uy1, oy1), (uy2, oy2))):
            for side in range(2):
                place = slice(0, 128) if side == 0 else slice(cols - 128, cols)
                n = 2 * which + side
                stage_y[n, k] = part[k, :, place] + both[:, 128 * n : 128 * n + 128]
                put(stage_y.at[n, k], out.at[k, 0, :, place], 2 + which)
    for n, (part, out) in enumerate(((ux1, ox1), (ux2, ox2), (uy1, oy1), (uy2, oy2))):
        pltpu.make_async_copy(part, out.at[:, 0], done.at[n]).wait()


def on_device(fields, metric_x, metric_y):
    count, _, rows, cols = fields.shape
    hbm = pl.BlockSpec(memory_space=pltpu.HBM)
    vmem = pl.BlockSpec(memory_space=pltpu.VMEM)
    block = pltpu.VMEM((count, rows, cols), F32)
    parts = pl.pallas_call(
        functools.partial(exchange, lax.axis_size("gx"), lax.axis_size("gy")),
        in_specs=[hbm] * 6,
        out_specs=[vmem] * 8,
        out_shape=[
            *[block] * 4,
            pltpu.VMEM((2, 24, cols), F32),
            pltpu.VMEM((2, 24, rows), F32),
            pltpu.VMEM((2, 24, cols), F32),
            pltpu.VMEM((2, 24, rows), F32),
        ],
        scratch_shapes=[
            pltpu.VMEM((count, rows, cols), F32),
            pltpu.VMEM((1, rows), F32),
            pltpu.VMEM((1, cols), F32),
            pltpu.VMEM((24, 128), F32),
            pltpu.VMEM((2, rows, 3 * rows), BF16),
            pltpu.VMEM((2, 2, 512, 256), BF16),
            pltpu.VMEM((9, rows, 128), F32),
            pltpu.SemaphoreType.DMA((5 + count,)),
            pltpu.SemaphoreType.DMA((4, CHUNKS)),
            pltpu.SemaphoreType.DMA((4, CHUNKS)),
            pltpu.SemaphoreType.REGULAR((2,)),
        ],
        compiler_params=pltpu.CompilerParams(collective_id=0, has_side_effects=True, vmem_limit_bytes=20 << 20),
        name="exchange",
    )(
        *(
            pltpu.with_memory_space_constraint(value, pltpu.HBM)
            for value in (
                fields,
                metric_x.reshape(1, rows),
                metric_y.reshape(1, cols),
                jnp.asarray(edge_rows(128)),
                jnp.asarray(line_tables(rows)),
                jnp.asarray(window_tables()),
            )
        )
    )
    return pl.pallas_call(
        join,
        in_specs=[vmem] * 10,
        out_specs=[hbm] * 4,
        out_shape=[jax.ShapeDtypeStruct(fields.shape, F32)] * 4,
        scratch_shapes=[
            pltpu.VMEM((2, count, rows, cols), F32),
            pltpu.VMEM((4, count, rows, 128), F32),
            pltpu.SemaphoreType.DMA((4,)),
        ],
        compiler_params=pltpu.CompilerParams(vmem_limit_bytes=20 << 20),
        name="join",
    )(*parts, jnp.asarray(face_tables_x(count, rows)), jnp.asarray(face_tables_y(128)))


def solution(mesh):
    whole = P(None, None, "gx", "gy")
    return jax.shard_map(
        on_device,
        mesh=mesh,
        in_specs=(whole, P("gx"), P("gy")),
        out_specs=(whole,) * 4,
        check_vma=False,
    )
```
